128 devices in a mesh: section: 4 (over y), expert: 32 (over x, z, core).
Axes of the slice: x: 4, y: 4, z: 4, core: 2. Of those that a mesh axis runs over, the one named last changes fastest.
Arguments:
- upstream_dy: bfloat16 [4, 2, 2048, 6144], P('section', None, 'expert'), may hold values from -6 to 6
- gate_logits: float32 [4, 2, 2048, 2], P('section', None, 'expert'), may hold values from -8 to 8
- expert_ids: int32 [4, 2, 2048, 2], P('section', None, 'expert'), may hold values from 0 to 3, all different within a row; in each aligned block of 64 rows (0 to 63, 64 to 127, ..., all dimensions but the last counted through in order) at most 36 rows name the same one
- saved_hidden: bfloat16 [4, 2, 32, 36, 32768], P('section', None, None, None, 'expert'), may hold values from -6 to 6
- down_weight: bfloat16 [4, 32768, 6144], P('section', 'expert'), may hold values from -0.0625 to 0.0625
- router_weight: float32 [4, 6144, 4], P('section'), may hold values from -0.078125 to 0.078125
Outputs:
- hidden_grad: bfloat16 [4, 2, 32, 36, 32768], P('section', None, None, None, 'expert')
- upstream_grad: bfloat16 [4, 2, 2048, 6144], P('section', None, 'expert')
The draws below stay inside these ranges and needn't reach their ends.
Inputs may be any that keep to these rules, and one draw needn't show every extreme that they name: `expert_ids`: the two experts of a token differ. In each device's block of 64 tokens of one microbatch no expert is named by more than 36 tokens, a bound that some block reaches.
All inputs are finite; a program needn't handle non-finite values.
Results may differ from the reference program's by a relative error of at most 0.0045.
Values may be sent and summed in bfloat16 or wider, within the bound.
A program may use at most 192 MiB of HBM per device.

```python
import math
import jax
import jax.numpy as jnp
import numpy as np
from jax import lax

D = 6144
FF_WIN = 8192
EXPERTS = 4
MICRO = 2
TOK_MB = 64
CAP = 36
SECTIONS = 4
SOURCES = 32
TOKENS = 2048


def levels(stream_key, dims, split, smallest, largest):
    gain, own = 1.0, jax.random.fold_in(stream_key, 6)
    for position, parts in split:
        draws = jnp.exp(jax.random.uniform(jax.random.fold_in(own, position), (parts,), jnp.float32, smallest / len(split), largest / len(split)))
        gain = gain * jnp.repeat(draws, dims[position] // parts).reshape([-1 if axis == position else 1 for axis in range(len(dims))])
    return gain


def assign_block(own_key, own, number, rows, number_of, top, bound, skew):
    ranking = jax.random.permutation(own_key, number_of)
    heavy_load, ordinary = load_shares(number_of, rows * top, bound, skew, True), load_shares(number_of, rows * top, bound, skew, False)
    places = jnp.arange(number_of)

    def named(lengths, rotation):
        used = int((lengths > 0).sum())
        fixed = max(1, used // 4)
        moved = fixed + (places - fixed + rotation * (used - fixed)) % max(1, number_of - fixed)
        return jnp.zeros((number_of,), jnp.int32).at[ranking[jnp.where(places < fixed, places, moved)]].set(jnp.asarray(lengths, jnp.int32))

    lengths = jnp.where(number % 4 == 0, named(heavy_load, number // 4), named(ordinary, number - number // 4 - 1))
    mixed = jax.random.permutation(jax.random.fold_in(own, 3), number_of)
    giver, taker = mixed[0:number_of // 2 * 2:2], mixed[1:number_of // 2 * 2:2]
    margin = jnp.minimum(lengths[giver] - 1, bound - lengths[taker]) // 2
    margin = jnp.where((giver == ranking[0]) | (taker == ranking[0]) | (lengths[taker] == 0), 0, jnp.maximum(margin, 0))
    moved = jax.random.randint(jax.random.fold_in(own, 4), (number_of // 2,), 0, 1 << 20) % (margin + 1)
    lengths = lengths.at[giver].add(-moved).at[taker].add(moved)
    members = jnp.searchsorted(jnp.cumsum(lengths), jnp.arange(rows * top), side="right").astype(jnp.int32)
    grid = members.reshape(top, rows).T
    grid = grid[jax.random.permutation(jax.random.fold_in(own, 1), rows)]
    rotation = jax.random.randint(jax.random.fold_in(own, 2), (rows, 1), 0, top)
    return jnp.take_along_axis(grid, (jnp.arange(top)[None, :] + rotation) % top, axis=1)


def load_shares(amount, total, reach, skew, full):
    portions = [(1 << 20) // math.isqrt(rank ** skew) + 1 for rank in range(1, amount + 1)]
    largest = reach if full else min(reach, max(-(-total // amount), total * portions[0] // sum(portions)))
    least = 1 if total - largest >= amount - 1 else 0
    counts, surplus = [largest] + [least] * (amount - 1), total - largest - least * (amount - 1)
    while surplus > 0:
        free = [i for i in range(1, amount) if counts[i] < largest] or [i for i in range(1, amount) if counts[i] < reach]
        whole, remaining = sum([portions[i] for i in free]), surplus
        for i in free:
            addition = min(reach - counts[i], max(1, remaining * portions[i] // whole), surplus)
            counts[i] = counts[i] + addition
            surplus = surplus - addition
    return np.array(counts)


def centred(own_key, dims, width, most, cuts=(), kind=jnp.bfloat16):
    array = width * jax.random.normal(own_key, dims, jnp.float32)
    if cuts:
        array = array * levels(own_key, dims, cuts, -0.22, 0.18)
    return jnp.clip(array, -most, most).astype(kind)


def setup_inputs(seed: int = 0) -> dict:
    splits = jax.random.split(jax.random.key(seed), 7)
    upstream_dy = centred(splits[0], (SECTIONS, MICRO, TOKENS, D), 1.0, 6.0, ((0, 4), (2, 32)))
    gate_logits = centred(splits[1], (SECTIONS, MICRO, TOKENS, 2), 1.5, 8.0, ((0, 4), (2, 32)), jnp.float32)
    expert_ids_keys = jax.random.split(jax.random.fold_in(splits[2], 1), SECTIONS * MICRO * TOKENS // TOK_MB)
    expert_ids_turns = jax.random.permutation(jax.random.fold_in(splits[2], 3), SECTIONS * MICRO * TOKENS // TOK_MB)
    expert_ids = jax.vmap(lambda own, number: assign_block(jax.random.fold_in(splits[2], 2), own, number, TOK_MB, EXPERTS, 2, CAP, 1))(expert_ids_keys, expert_ids_turns).reshape((SECTIONS, MICRO, TOKENS, 2))
    saved_hidden = centred(splits[3], (SECTIONS, MICRO, SOURCES, CAP, EXPERTS * FF_WIN), 1.0, 6.0, ((0, 4), (4, 32)))
    down_weight = centred(splits[4], (SECTIONS, EXPERTS * FF_WIN, D), FF_WIN ** -0.5, 0.0625, ((0, 4), (1, 32)))
    router_weight = centred(splits[5], (SECTIONS, D, EXPERTS), D ** -0.5, 0.078125, ((0, 4),), jnp.float32)
    return {"upstream_dy": upstream_dy, "gate_logits": gate_logits, "expert_ids": expert_ids, "saved_hidden": saved_hidden, "down_weight": down_weight, "router_weight": router_weight}


def reference(upstream_dy, gate_logits, expert_ids, saved_hidden, down_weight, router_weight):
    highest = lax.Precision.HIGHEST
    expert_range = jnp.arange(EXPERTS, dtype=jnp.int32)
    slot_index = jnp.arange(CAP).astype(jnp.float32)
    section_grads = []
    section_inputs = []
    for section_id in range(SECTIONS):
        micro_grads = []
        micro_inputs = []
        for micro_id in range(MICRO):
            out_grad = upstream_dy[section_id, micro_id]
            logits = gate_logits[section_id, micro_id]
            gate_prob = jax.nn.sigmoid(logits - logits[:, ::-1])
            onehot = (expert_ids[section_id, micro_id][:, :, None] == expert_range).astype(jnp.float32)
            picked = jnp.sum(onehot, axis=1).reshape(SOURCES, TOK_MB, EXPERTS)
            slot_rank = jnp.cumsum(picked, axis=1) - picked
            select = picked[:, None] * (slot_rank[:, None] == slot_index[None, :, None, None]).astype(jnp.float32)
            copies = jnp.einsum("scte,std->escd", select, out_grad.astype(jnp.float32).reshape(SOURCES, TOK_MB, D), precision=highest).astype(jnp.bfloat16)
            gate_expert = jnp.sum(onehot * gate_prob[:, :, None], axis=1).reshape(SOURCES, TOK_MB, EXPERTS)
            slot_gate = jnp.einsum("scte,ste->esc", select, gate_expert, precision=highest).astype(jnp.bfloat16)
            slot_gate = lax.optimization_barrier(slot_gate).astype(jnp.float32)
            grads_list = []
            partial_list = []
            for expert_id in range(EXPERTS):
                weight = down_weight[section_id, expert_id * FF_WIN:(expert_id + 1) * FF_WIN]
                hidden_raw = jnp.dot(copies[expert_id].reshape(SOURCES * CAP, D), weight.T, preferred_element_type=jnp.float32).reshape(SOURCES, CAP, FF_WIN)
                grads_list.append((slot_gate[expert_id][:, :, None] * hidden_raw).astype(jnp.bfloat16))
                saved = saved_hidden[section_id, micro_id, :, :, expert_id * FF_WIN:(expert_id + 1) * FF_WIN].astype(jnp.float32)
                partial_list.append(jnp.sum(hidden_raw * saved, axis=-1))
            micro_grads.append(jnp.concatenate(grads_list, axis=-1))
            per_expert = jnp.stack(partial_list)
            token_part = jnp.einsum("scte,esc->ste", select, per_expert, precision=highest).reshape(TOKENS, EXPERTS)
            pair_part = jnp.sum(onehot * token_part[:, None, :], axis=-1)
            mixed = jnp.sum(gate_prob * pair_part, axis=-1, keepdims=True)
            logit_grad = gate_prob * (pair_part - mixed)
            spread = jnp.sum(onehot * logit_grad[:, :, None], axis=1)
            router_term = jnp.dot(spread, router_weight[section_id].T, precision=highest)
            micro_inputs.append((out_grad.astype(jnp.float32) + router_term).astype(jnp.bfloat16))
        section_grads.append(jnp.stack(micro_grads))
        section_inputs.append(jnp.stack(micro_inputs))
    hidden_grad = jnp.stack(section_grads)
    inputs_all = jnp.stack(section_inputs)
    upstream_grad = jnp.concatenate([inputs_all[1:], jnp.zeros_like(inputs_all[:1])], axis=0)
    return (hidden_grad, upstream_grad)
```

```python
import functools

import jax
import jax.numpy as jnp
from jax import lax
from jax.experimental import pallas as pl
from jax.experimental.pallas import tpu as pltpu
from jax.sharding import PartitionSpec as P

EXPERTS = 4
CAP = 36
NX = 4
NZ = 4
NC = 6
SRC = 2
ROWS = 16
MESH = pl.DeviceIdType.MESH
F32 = jnp.float32
BF16 = jnp.bfloat16


def permutation():
    i = lax.broadcasted_iota(jnp.int32, (256, 256), 0)
    n = lax.broadcasted_iota(jnp.int32, (256, 256), 1)
    z, x, src, slot = i >> 6, (i >> 4) & 3, (i >> 3) & 1, i & 7
    return (n == slot * 32 + (x * 4 + z) * 2 + src).astype(F32).astype(BF16)


def expert_kernel(
    groups, width, x_hbm, ct_hbm, saved_hbm, w_hbm, grad_hbm, part_ref,
    rows, wv, acc, sv, x2, ct2, sel, packed, gs, gt,
    x_sem, w_sem, s_sem, o_sem, loc_sem, b0_send, b0_recv, xs, xr, zs, zr, bs, br,
):
    me = lax.axis_index("expert")
    mx, mz, mc = me // 8, (me // 2) % 4, me % 2
    half = width * NC

    def dev(x, z, c):
        return {"expert": (lax.rem(x + 8, NX) * NZ + lax.rem(z + 8, NZ)) * 2 + c}

    sibling = dev(mx, mz, 1 - mc)
    xdev = [dev(mx + d, mz, mc) for d in range(NX)]
    zup, zdown = dev(mx, mz + 1, mc), dev(mx, mz - 1, mc)

    barrier = pltpu.get_barrier_semaphore()
    for target in (sibling, xdev[1], xdev[2], xdev[3], zup, zdown):
        pl.semaphore_signal(barrier, inc=1, device_id=target, device_id_type=MESH)
    pl.semaphore_wait(barrier, 6)

    def remote(src, dst, send, recv, target):
        return pltpu.make_async_remote_copy(
            src_ref=src, dst_ref=dst, send_sem=send, recv_sem=recv, device_id=target, device_id_type=MESH
        )

    mine = pl.ds(pl.multiple_of(mc * half, 128), half)
    other = pl.ds(pl.multiple_of((1 - mc) * half, 128), half)
    mine_rows = pl.ds(pl.multiple_of(mc * 128, 128), 128)
    sib_rows = pl.ds(pl.multiple_of((1 - mc) * 128, 128), 128)
    swap_x = remote(x_hbm.at[:, other], x2.at[mine_rows, :], b0_send.at[0], b0_recv.at[0], sibling)
    swap_c = remote(ct_hbm, ct2.at[mc], b0_send.at[1], b0_recv.at[1], sibling)
    own_x = pltpu.make_async_copy(x_hbm.at[:, mine], x2.at[mine_rows, :], x_sem.at[0])
    own_c = pltpu.make_async_copy(ct_hbm, ct2.at[mc], x_sem.at[1])
    for copy in (swap_c, swap_x, own_c, own_x):
        copy.start()
    w_copy = {}
    for k in range(NC):
        for h in range(2):
            cols = pl.ds(h * half + k * width, width)
            w_copy[k, h] = pltpu.make_async_copy(w_hbm.at[:, cols], wv.at[:, cols], w_sem.at[k, h])
            w_copy[k, h].start()
    s_copy = [pltpu.make_async_copy(saved_hbm.at[g], sv.at[g], s_sem.at[g]) for g in range(groups)]
    for copy in s_copy:
        copy.start()

    gs[...] = jnp.zeros_like(gs)
    own_c.wait()
    swap_c.wait_recv()
    for e in range(EXPERTS):
        code = jnp.concatenate([ct2[0, e : e + 1, :], ct2[1, e : e + 1, :]], axis=1)
        gate = jnp.concatenate([ct2[0, 4 + e : 5 + e, :], ct2[1, 4 + e : 5 + e, :]], axis=1)
        row = lax.broadcasted_iota(jnp.int32, (groups * ROWS, 256), 0).astype(F32)
        chosen = (row == code).astype(F32).astype(BF16)
        sel[e] = chosen
        gs[e, :, 0 : groups * ROWS] = lax.dot_general(
            jnp.broadcast_to(gate, (8, 256)).astype(BF16), chosen, (((1,), (1,)), ((), ())),
            preferred_element_type=F32,
        )
    own_x.wait()
    swap_x.wait_recv()

    chip = mz * NX + mx

    def group(k, h, z):
        return rows.at[k, h, :, pl.ds(lax.rem(z + 8, NZ) * NX, NX)]

    def gate_group(z):
        return gt.at[pl.ds(lax.rem(z + 8, NZ) * NX, NX)]

    def pack(k):
        for e in range(EXPERTS):
            block = jnp.dot(sel[e], x2[:, k * width : (k + 1) * width], preferred_element_type=F32)
            packed[k, e] = block.astype(BF16).reshape(groups, ROWS, width)

    waits = []

    def start_x(k):
        local = pltpu.make_async_copy(packed.at[k, mx], rows.at[k, mc, :, chip], loc_sem.at[k])
        local.start()
        for d in (2, 1, 3):
            e = lax.rem(mx + d, NX)
            copy = remote(packed.at[k, e], rows.at[k, mc, :, chip], xs.at[k, d - 1], xr.at[k, d - 1], xdev[d])
            copy.start()
            waits.append(copy)
        return local

    def arrived(ref, sem):
        remote(ref, ref, bs.at[0, 0], sem, sibling).wait_recv()

    def to_sibling(k, which, z):
        copy = remote(group(k, mc, z), group(k, mc, z), bs.at[k, which], br.at[k, which], sibling)
        copy.start()
        waits.append(copy)

    def z_send(ref, k, which, target):
        copy = remote(ref, ref, zs.at[k, which], zr.at[k, which], target)
        copy.start()
        waits.append(copy)

    def gates_x():
        local = pltpu.make_async_copy(gs.at[mx], gt.at[chip], loc_sem.at[NC])
        local.start()
        for d in (1, 2, 3):
            e = lax.rem(mx + d, NX)
            copy = remote(gs.at[e], gt.at[chip], xs.at[NC, d - 1], xr.at[NC, d - 1], xdev[d])
            copy.start()
            waits.append(copy)
        return local

    def stage_b(k, local):
        local.wait()
        for d in (1, 2, 3):
            source = mz * NX + lax.rem(mx - d + NX, NX)
            ref = rows.at[k, mc, :, source] if k < NC else gt.at[source]
            arrived(ref, xr.at[k, d - 1])
        ref = group(k, mc, mz) if k < NC else gate_group(mz)
        z_send(ref, k, 0, zup)
        z_send(ref, k, 1, zdown)
        if k < NC:
            to_sibling(k, 0, mz)

    def stage_c(k):
        below = group(k, mc, mz - 1) if k < NC else gate_group(mz - 1)
        above = group(k, mc, mz + 1) if k < NC else gate_group(mz + 1)

        def take_below():
            arrived(below, zr.at[k, 0])
            if k % 2 == 0:
                z_send(below, k, 2, zup)
            if k < NC:
                to_sibling(k, 1, mz - 1)

        def take_above():
            arrived(above, zr.at[k, 1])
            if k % 2 == 1:
                z_send(above, k, 2, zdown)
            if k < NC:
                to_sibling(k, 2, mz + 1)

        take_below()
        take_above()

    def stage_d(k):
        arrived(group(k, mc, mz + 2) if k < NC else gate_group(mz + 2), zr.at[k, 2])
        if k < NC:
            to_sibling(k, 3, mz + 2)

    big = groups // 3

    def compute(k):
        for which, z in enumerate((mz, mz - 1, mz + 1, mz + 2)):
            arrived(group(k, 1 - mc, z), br.at[k, which])
        for h in range(2):
            w_copy[k, h].wait()

        def body(m, carry):
            at = pl.ds(m * big, big)
            total = None
            for h in range(2):
                left = rows[k, h, at].reshape(big * 256, width)
                right = wv[:, h * half + k * width : h * half + (k + 1) * width]
                term = lax.dot_general(left, right, (((1,), (1,)), ((), ())), preferred_element_type=F32)
                total = term if total is None else total + term
            total = total.reshape(big, 256, total.shape[-1])
            acc[at] = total if k == 0 else acc[at] + total
            return carry

        lax.fori_loop(0, 3, body, 0)

    pack(0)
    pack(1)
    locals_ = {0: start_x(0)}
    locals_[NC] = gates_x()
    locals_[1] = start_x(1)
    for k in range(2, NC):
        pack(k)
        locals_[k] = start_x(k)
    perm = permutation()

    def place_saved(g, carry):
        sv[g] = jnp.dot(perm, sv[g], preferred_element_type=F32).astype(BF16)
        return carry

    for step in range(NC + 3):
        if step < NC:
            stage_b(step, locals_[step])
        if step == 1:
            stage_b(NC, locals_[NC])
        if 0 <= step - 1 < NC:
            stage_c(step - 1)
        if step == 2:
            stage_c(NC)
        if 0 <= step - 2 < NC:
            stage_d(step - 2)
        if step == 3:
            stage_d(NC)
        if step == 0:
            for copy in s_copy:
                copy.wait()
            lax.fori_loop(0, groups, place_saved, 0)
        if 0 <= step - 3 < NC:
            compute(step - 3)

    lane = lax.broadcasted_iota(jnp.int32, (256, 256), 1)
    row16 = lax.broadcasted_iota(jnp.int32, (256, 256), 0) & 15
    gates = jnp.broadcast_to(gt[:, 0:1, :], (16, 16, 256)).reshape(256, 256)
    part_ref[...] = jnp.zeros_like(part_ref)

    def finish(g, carry):
        place = lane == row16 + g * 16
        gate = jnp.sum(jnp.where(place, gates, 0.0), axis=1, keepdims=True)
        raw = acc[g]
        dots = jnp.sum(raw * sv[g].astype(F32), axis=1, keepdims=True)
        sv[g] = (gate * raw).astype(BF16)
        pltpu.make_async_copy(sv.at[g], grad_hbm.at[g], o_sem.at[g]).start()
        spread = jnp.where(place, dots, 0.0).reshape(16, 16, 256)
        part_ref[...] += jnp.sum(spread, axis=1)
        return carry

    lax.fori_loop(0, groups, finish, 0)
    for g in range(groups):
        pltpu.make_async_copy(sv.at[g], grad_hbm.at[g], o_sem.at[g]).wait()
    swap_c.wait_send()
    swap_x.wait_send()
    for copy in waits:
        copy.wait_send()


def expert_call(tokens, codes, saved, weight):
    depth, hidden = tokens.shape[-1], weight.shape[0]
    groups = saved.shape[0]
    width = depth // 2 // NC
    dma = pltpu.SemaphoreType.DMA
    return pl.pallas_call(
        functools.partial(expert_kernel, groups, width),
        name="experts",
        out_shape=(
            jax.ShapeDtypeStruct((groups, 256, hidden), BF16),
            jax.ShapeDtypeStruct((16, 256), F32),
        ),
        in_specs=[pl.BlockSpec(memory_space=pl.ANY)] * 4,
        out_specs=(pl.BlockSpec(memory_space=pl.ANY), pl.BlockSpec(memory_space=pltpu.VMEM)),
        scratch_shapes=[
            pltpu.VMEM((NC, 2, groups, 16, ROWS, width), BF16),
            pltpu.VMEM((hidden, depth), BF16),
            pltpu.VMEM((groups, 256, hidden), F32),
            pltpu.VMEM((groups, 256, hidden), BF16),
            pltpu.VMEM((256, depth // 2), BF16),
            pltpu.VMEM((2, 8, 128), F32),
            pltpu.VMEM((EXPERTS, groups * ROWS, 256), BF16),
            pltpu.VMEM((NC, EXPERTS, groups, ROWS, width), BF16),
            pltpu.VMEM((EXPERTS, 8, 256), F32),
            pltpu.VMEM((16, 8, 256), F32),
            dma((2,)), dma((NC, 2)), dma((groups,)), dma((groups,)), dma((NC + 1,)), dma((2,)), dma((2,)),
            dma((NC + 1, 3)), dma((NC + 1, 3)), dma((NC + 1, 3)), dma((NC + 1, 3)), dma((NC, 4)), dma((NC, 4)),
        ],
        compiler_params=pltpu.CompilerParams(
            collective_id=0, has_side_effects=True, vmem_limit_bytes=67043328
        ),
        cost_estimate=pl.CostEstimate(
            flops=2 * groups * 256 * depth * hidden, bytes_accessed=200_000_000, transcendentals=0
        ),
    )(tokens, codes, saved, weight)


def place_kernel(grad_ref, out_ref):
    turned = lax.dot_general(
        permutation(), grad_ref[0], (((0,), (0,)), ((), ())), preferred_element_type=F32
    )
    out_ref[0] = turned.astype(BF16)


def place_call(grad):
    groups, rows, hidden = grad.shape
    spec = pl.BlockSpec((1, rows, hidden), lambda g: (g, 0, 0))
    return pl.pallas_call(
        place_kernel,
        name="place",
        grid=(groups,),
        out_shape=jax.ShapeDtypeStruct(grad.shape, BF16),
        in_specs=[spec],
        out_specs=spec,
    )(grad)


def passed_along(value):
    count = lax.axis_size("section")
    return lax.ppermute(value, "section", [(source, source - 1) for source in range(1, count)])


def local(upstream_dy, gate_logits, expert_ids, saved_hidden, down_weight, router_weight):
    highest = lax.Precision.HIGHEST
    micro, per, depth = upstream_dy.shape[1:]
    hidden = down_weight.shape[1]
    logits, chosen, out_grad = gate_logits[0], expert_ids[0], upstream_dy[0]
    gate_prob = jax.nn.sigmoid(logits - logits[..., ::-1])
    onehot = (chosen[..., None] == jnp.arange(EXPERTS, dtype=jnp.int32)).astype(F32)
    picked = jnp.sum(onehot, axis=2)
    earlier = (jnp.arange(per)[:, None] > jnp.arange(per)[None, :]).astype(F32)
    slot = jnp.einsum("ts,mse->mte", earlier, picked) + (jnp.arange(micro) * CAP).astype(F32)[:, None, None]
    gate = jnp.sum(onehot * gate_prob[..., None], axis=2)
    core = lax.rem(lax.axis_index("expert"), SRC).astype(F32)
    base = jnp.floor(slot / 8)
    code = jnp.where(picked > 0, base * 16 + core * 8 + (slot - base * 8), -1.0)
    flat = micro * per
    codes = jnp.concatenate(
        [code.reshape(flat, EXPERTS).T, gate.astype(BF16).astype(F32).reshape(flat, EXPERTS).T]
    )
    saved = saved_hidden[0].transpose(0, 2, 1, 3).reshape(micro * CAP // 8, 256, hidden)
    next_grad = passed_along(out_grad)
    next_router = passed_along(router_weight[0])
    grad, part = expert_call(out_grad.reshape(flat, depth), codes, saved, down_weight[0])
    part = part[:, : micro * CAP * SRC].reshape(NZ, NX, micro * CAP // 8, SRC, 8)
    part = part.transpose(1, 0, 3, 2, 4).reshape(NX * NZ * SRC, micro * CAP)
    returned = lax.all_to_all(part, "expert", split_axis=0, concat_axis=0, tiled=True)
    per_expert = jnp.sum(returned.reshape(EXPERTS, NZ * SRC, micro * CAP), axis=1)
    slots = jnp.arange(micro * CAP).astype(F32)
    select = picked[..., None] * (slot[..., None] == slots).astype(F32)
    token_part = jnp.einsum("mtec,ec->mte", select, per_expert, precision=highest)
    pair_part = jnp.sum(onehot * token_part[:, :, None, :], axis=-1)
    mixed = jnp.sum(gate_prob * pair_part, axis=-1, keepdims=True)
    logit_grad = gate_prob * (pair_part - mixed)
    spread = jnp.sum(onehot * logit_grad[..., None], axis=2)
    spread = passed_along(spread)
    router_term = jnp.einsum("mte,de->mtd", spread, next_router, precision=highest)
    upstream = (next_grad.astype(F32) + router_term).astype(BF16)
    hidden_grad = place_call(grad).reshape(micro, CAP, NX * NZ * SRC, hidden).transpose(0, 2, 1, 3)
    return (hidden_grad[None], upstream[None])


def solution(mesh):
    placed = (
        P("section", None, "expert", None),
        P("section", None, "expert", None),
        P("section", None, "expert", None),
        P("section", None, None, None, "expert"),
        P("section", "expert", None),
        P("section", None, None),
    )
    return jax.shard_map(
        local,
        mesh=mesh,
        in_specs=placed,
        out_specs=(P("section", None, None, None, "expert"), P("section", None, "expert", None)),
        check_vma=False,
    )
```

```python
import functools

import jax
import jax.numpy as jnp
from jax import lax
from jax.experimental import pallas as pl
from jax.experimental.pallas import tpu as pltpu
from jax.sharding import PartitionSpec as P

EXPERTS = 4
CAP = 36
NX = 4
NZ = 4
NC = 12
A_CHUNKS = (0, 1, 2, 3, 4, 5, 6)
B_CHUNKS = (7, 8, 9, 10, 11)
ORDER = ((0, 7), (1, 8), (2, 3), (9, 4), (10,), (5,), (11,), (6,))
ROWS = 16
MESH = pl.DeviceIdType.MESH
F32 = jnp.float32
BF16 = jnp.bfloat16
NT = (((1,), (1,)), ((), ()))
HIGHEST = lax.Precision.HIGHEST


def permutation(turned):
    i = lax.broadcasted_iota(jnp.int32, (256, 256), 1 if turned else 0)
    n = lax.broadcasted_iota(jnp.int32, (256, 256), 0 if turned else 1)
    z, x, src, slot = i >> 6, (i >> 4) & 3, (i >> 3) & 1, i & 7
    return (n == slot * 32 + (x * 4 + z) * 2 + src).astype(F32).astype(BF16)


def codes_of(tile, src):
    picks = [(tile[0:1] == e).astype(F32) for e in range(EXPERTS)], [(tile[1:2] == e).astype(F32) for e in range(EXPERTS)]
    picked = jnp.concatenate([a + b for a, b in zip(*picks)] * 2, axis=0)
    t = lax.broadcasted_iota(jnp.int32, (128, 128), 0)
    u = lax.broadcasted_iota(jnp.int32, (128, 128), 1)
    earlier = ((t < u) & ((t >> 6) == (u >> 6))).astype(F32).astype(BF16)
    rank = jnp.dot(picked.astype(BF16), earlier, preferred_element_type=F32)
    micro = (lax.broadcasted_iota(jnp.int32, (8, 128), 1) >> 6).astype(F32)
    slot = rank + micro * CAP
    base = jnp.floor(slot * 0.125)
    code = jnp.where(picked > 0, base * 8 + slot + src * 8, -1.0)
    diff = tile[2:3] - tile[3:4]
    first, second = jax.nn.sigmoid(diff), jax.nn.sigmoid(-diff)
    gate = jnp.concatenate([a * first + b * second for a, b in zip(*picks)] * 2, axis=0)
    return code, gate


def expert_kernel(
    groups, width, x_hbm, info_hbm, saved_hbm, w_hbm, router_hbm, grad_hbm, next_hbm, nrouter_hbm, spread_ref,
    rows, wv, acc, sv, x2, info, selz, packed, raw_z, packed_z, gs, gt, own_gate, pts, pr, sums, spread,
    x_sem, w_sem, s_sem, o_sem, loc_sem, b0_send, b0_recv, xs, xr, zs, zr, bs, br, ps, pr_sem,
):
    me = lax.axis_index("expert")
    section = lax.axis_index("section")
    mx, mz, mc = me // 8, (me // 2) % 4, me % 2
    half = width * NC

    def dev(x, z, c, s=0):
        index = (lax.rem(x + 8, NX) * NZ + lax.rem(z + 8, NZ)) * 2 + c
        return (lax.rem(section + s + 4, 4), index)

    sibling = dev(mx, mz, 1 - mc)
    xdev = [dev(mx + d, mz, mc) for d in range(NX)]
    zdev = [dev(mx, mz + d, mc) for d in range(NZ)]
    before, after = dev(mx, mz, mc, -1), dev(mx, mz, mc, 1)
    chips = [(dx, dz) for dx in range(NX) for dz in range(NZ) if dx or dz]

    barrier = pltpu.get_barrier_semaphore()
    partners = [sibling, before, after] + [dev(mx + dx, mz + dz, mc) for dx, dz in chips]
    for target in partners:
        pl.semaphore_signal(barrier, inc=1, device_id=target, device_id_type=MESH)
    pl.semaphore_wait(barrier, len(partners))

    def remote(src, dst, send, recv, target):
        return pltpu.make_async_remote_copy(
            src_ref=src, dst_ref=dst, send_sem=send, recv_sem=recv, device_id=target, device_id_type=MESH
        )

    waits = []

    def send(src, dst, send_sem, recv_sem, target):
        copy = remote(src, dst, send_sem, recv_sem, target)
        copy.start()
        waits.append(copy)

    def arrived(ref, sem):
        remote(ref, ref, b0_send.at[0], sem, sibling).wait_recv()

    mine = pl.ds(pl.multiple_of(mc * half, 128), half)
    other = pl.ds(pl.multiple_of((1 - mc) * half, 128), half)
    mine_rows = pl.ds(pl.multiple_of(mc * 128, 128), 128)
    sib_rows = pl.ds(pl.multiple_of((1 - mc) * 128, 128), 128)
    send(info_hbm, info.at[mz, mc], b0_send.at[1], b0_recv.at[1], sibling)
    send(x_hbm.at[:, other], x2.at[mine_rows, :], b0_send.at[0], b0_recv.at[0], sibling)
    own_x = pltpu.make_async_copy(x_hbm.at[:, mine], x2.at[mine_rows, :], x_sem.at[0])
    own_c = pltpu.make_async_copy(info_hbm, info.at[mz, mc], x_sem.at[1])
    own_c.start()
    own_x.start()

    order = [k for ks in ORDER for k in ks]

    def w_copies(i):
        copies = []
        for n, k in enumerate(ORDER[i]):
            for h in range(2):
                cols = pl.ds(h * half + k * width, width)
                copies.append(
                    pltpu.make_async_copy(w_hbm.at[:, cols], wv.at[i % 2, n * 2 + h], w_sem.at[i % 2, n * 2 + h])
                )
        return copies

    for i in range(2):
        for copy in w_copies(i):
            copy.start()
    s_copy = [pltpu.make_async_copy(saved_hbm.at[g], sv.at[g], s_sem.at[g]) for g in range(groups)]
    for copy in s_copy:
        copy.start()
    send(x_hbm, next_hbm, b0_send.at[2], b0_recv.at[2], before)
    send(router_hbm, nrouter_hbm, b0_send.at[3], b0_recv.at[3], before)

    def select(z):
        code0, gate0 = codes_of(info[z, 0], 0)
        code1, gate1 = codes_of(info[z, 1], 1)
        row = lax.broadcasted_iota(jnp.int32, (groups * ROWS, 256), 0).astype(F32)
        gates = []
        for e in range(EXPERTS):
            code = jnp.concatenate([code0[e : e + 1], code1[e : e + 1]], axis=1)
            selz[z, e] = (row == code).astype(F32).astype(BF16)
            gates.append(jnp.concatenate([gate0[e : e + 1], gate1[e : e + 1]], axis=1))
        return gates, gate0, gate1

    gs[...] = jnp.zeros_like(gs)
    own_c.wait()
    arrived(info.at[mz, 1 - mc], b0_recv.at[1])
    for d in (1, 3, 2):
        send(info.at[mz], info.at[mz], zs.at[NC + 1, d - 1], zr.at[NC + 1, d - 1], zdev[d])
    gates, gate0, gate1 = select(mz)
    own_gate[...] = jnp.where(mc == 0, gate0, gate1)
    for e in range(EXPERTS):
        gs[e, :, 0 : groups * ROWS] = lax.dot_general(
            jnp.broadcast_to(gates[e], (8, 256)).astype(BF16), selz[mz, e], NT, preferred_element_type=F32
        )
    own_x.wait()
    arrived(x2.at[sib_rows, :], b0_recv.at[0])

    def columns(k):
        return slice(k * width, (k + 1) * width)

    def start_raw(k):
        b = B_CHUNKS.index(k)
        for d in (1, 3, 2):
            send(x2.at[:, columns(k)], raw_z.at[b, mz], zs.at[k, d - 1], zr.at[k, d - 1], zdev[d])

    def pack(k):
        a = A_CHUNKS.index(k)
        for e in range(EXPERTS):
            block = jnp.dot(selz[mz, e], x2[:, columns(k)], preferred_element_type=F32)
            packed[a, e] = block.astype(BF16).reshape(groups, ROWS, width)

    locals_ = {}

    def start_x(k):
        if k == NC:
            here = gs.at
            there = gt.at[mz, mx]
        elif k in A_CHUNKS:
            here = packed.at[A_CHUNKS.index(k)].at
            there = rows.at[k, mc, :, mz, mx]
        else:
            here = packed_z.at[B_CHUNKS.index(k)].at
            there = rows.at[k, mc, :, :, mx]
        locals_[k] = pltpu.make_async_copy(here[mx], there, loc_sem.at[k])
        locals_[k].start()
        for d in (2, 1, 3):
            send(here[lax.rem(mx + d, NX)], there, xs.at[k, d - 1], xr.at[k, d - 1], xdev[d])

    def wait_x(k):
        locals_[k].wait()
        for d in (1, 2, 3):
            x = lax.rem(mx - d + NX, NX)
            if k == NC:
                ref = gt.at[mz, x]
            elif k in A_CHUNKS:
                ref = rows.at[k, mc, :, mz, x]
            else:
                ref = rows.at[k, mc, :, :, x]
            arrived(ref, xr.at[k, d - 1])

    def around_z(k):
        wait_x(k)
        ref = gt.at[mz] if k == NC else rows.at[k, mc, :, mz]
        for d in (1, 3, 2):
            send(ref, ref, zs.at[k, d - 1], zr.at[k, d - 1], zdev[d])
        if k < NC:
            send(ref, ref, bs.at[k, 0], br.at[k, 0], sibling)

    def cross_x(k):
        b = B_CHUNKS.index(k)
        for d in range(NZ):
            z = lax.rem(mz + d, NZ)
            if d:
                arrived(raw_z.at[b, z], zr.at[k, NZ - d - 1])
            tokens = raw_z[b, z] if d else x2[:, columns(k)]
            for e in range(EXPERTS):
                block = jnp.dot(selz[z, e], tokens, preferred_element_type=F32)
                packed_z[b, e, :, z] = block.astype(BF16).reshape(groups, ROWS, width)
        start_x(k)

    def take(k):
        if k in A_CHUNKS:
            for d in (1, 3, 2):
                ref = rows.at[k, mc, :, lax.rem(mz - d + NZ, NZ)]
                arrived(ref, zr.at[k, d - 1])
                send(ref, ref, bs.at[k, d], br.at[k, d], sibling)
        else:
            wait_x(k)
            send(rows.at[k, mc], rows.at[k, mc], bs.at[k, 0], br.at[k, 0], sibling)

    def shared(k):
        if k in A_CHUNKS:
            for d in range(NZ):
                arrived(rows.at[k, 1 - mc, :, lax.rem(mz - d + NZ, NZ)], br.at[k, d])
        else:
            arrived(rows.at[k, 1 - mc], br.at[k, 0])

    big = groups // 3

    def compute(i):
        for k in ORDER[i]:
            shared(k)
        for copy in w_copies(i):
            copy.wait()

        def body(m, carry):
            at = pl.ds(m * big, big)
            total = None
            for n, k in enumerate(ORDER[i]):
                for h in range(2):
                    left = rows[k, h, at].reshape(big * 256, width)
                    term = lax.dot_general(left, wv[i % 2, n * 2 + h], NT, preferred_element_type=F32)
                    total = term if total is None else total + term
            total = total.reshape(big, 256, total.shape[-1])
            acc[at] = total if i == 0 else acc[at] + total
            return carry

        lax.fori_loop(0, 3, body, 0)
        if i + 2 < len(ORDER):
            for copy in w_copies(i + 2):
                copy.start()

    start_x(NC)
    for n, k in enumerate(A_CHUNKS):
        pack(k)
        if n:
            start_x(A_CHUNKS[n - 1])
        if n < len(B_CHUNKS):
            start_raw(B_CHUNKS[n])
    start_x(A_CHUNKS[-1])
    around_z(NC)
    for d in (1, 2, 3):
        z = lax.rem(mz + d, NZ)
        arrived(info.at[z], zr.at[NC + 1, NZ - d - 1])
        select(z)
    for n, k in enumerate(A_CHUNKS):
        around_z(k)
        if n < len(B_CHUNKS):
            cross_x(B_CHUNKS[n])
    perm = permutation(False)

    def place_saved(g, carry):
        sv[g] = jnp.dot(perm, sv[g], preferred_element_type=F32).astype(BF16)
        return carry

    for copy in s_copy:
        copy.wait()
    lax.fori_loop(0, groups, place_saved, 0)
    for d in (1, 2, 3):
        arrived(gt.at[lax.rem(mz - d + NZ, NZ)], zr.at[NC, d - 1])
    for i, ks in enumerate(ORDER):
        for k in ks:
            take(k)
        if i:
            compute(i - 1)
    compute(len(ORDER) - 1)

    lane = lax.broadcasted_iota(jnp.int32, (256, 256), 1)
    row16 = lax.broadcasted_iota(jnp.int32, (256, 256), 0) & 15

    def dots(g, total):
        raw = acc[g]
        part = jnp.sum(raw * sv[g].astype(F32), axis=1, keepdims=True)
        part = jnp.where(lane == row16 + g * 16, part, 0.0).reshape(16, 16, 256)
        return total + jnp.sum(part, axis=1)

    part = lax.fori_loop(0, groups, dots, jnp.zeros((16, 256), F32))
    pts[...] = jnp.broadcast_to(part[:, None, :], (16, 8, 256))
    slot = mx * NZ + mz
    own_part = pltpu.make_async_copy(pts.at[mz * NX + mx], pr.at[slot], loc_sem.at[NC + 1])
    own_part.start()
    for n, (dx, dz) in enumerate(chips):
        x, z = lax.rem(mx + dx, NX), lax.rem(mz + dz, NZ)
        send(pts.at[z * NX + x], pr.at[slot], ps.at[n], pr_sem.at[n], dev(x, z, mc))

    gates = jnp.broadcast_to(gt[...].reshape(16, 8, 256)[:, 0:1, :], (16, 16, 256)).reshape(256, 256)

    def finish(g, carry):
        gate = jnp.sum(jnp.where(lane == row16 + g * 16, gates, 0.0), axis=1, keepdims=True)
        sv[g] = (gate * acc[g]).astype(BF16)
        pltpu.make_async_copy(sv.at[g], grad_hbm.at[g], o_sem.at[g]).start()
        return carry

    lax.fori_loop(0, groups, finish, 0)

    own_part.wait()
    for n, (dx, dz) in enumerate(chips):
        x, z = lax.rem(mx - dx + NX, NX), lax.rem(mz - dz + NZ, NZ)
        arrived(pr.at[x * NZ + z], pr_sem.at[n])
    summed = jnp.sum(pr[...].reshape(EXPERTS, NZ, 8, 256), axis=1)
    sums[0] = summed
    send(sums.at[0], sums.at[1], bs.at[NC, 0], br.at[NC, 0], sibling)
    arrived(sums.at[1], br.at[NC, 0])
    summed = summed + sums[1]
    token = []
    for e in range(EXPERTS):
        chosen = jnp.where(mc == 0, selz[mz, e, :, 0:128].astype(F32), selz[mz, e, :, 128:256].astype(F32))
        token.append(
            jnp.dot(summed[e, :, 0 : groups * ROWS], chosen, preferred_element_type=F32, precision=HIGHEST)[0:1]
        )
    token = jnp.concatenate(token * 2, axis=0)
    gate = own_gate[...]
    mixed = jnp.sum((gate * token)[0:EXPERTS], axis=0, keepdims=True)
    spread[0] = gate * (token - mixed)
    send(spread.at[0], spread.at[1], b0_send.at[4], b0_recv.at[4], before)
    for g in range(groups):
        pltpu.make_async_copy(sv.at[g], grad_hbm.at[g], o_sem.at[g]).wait()
    arrived(next_hbm, b0_recv.at[2])
    arrived(nrouter_hbm, b0_recv.at[3])
    arrived(spread.at[1], b0_recv.at[4])
    spread_ref[...] = spread[1]
    for copy in waits:
        copy.wait_send()


def expert_call(tokens, info, saved, weight, router):
    depth, hidden = tokens.shape[-1], weight.shape[0]
    groups = saved.shape[0]
    width = depth // 2 // NC
    dma = pltpu.SemaphoreType.DMA
    anywhere = pl.BlockSpec(memory_space=pl.ANY)
    na, nb = len(A_CHUNKS), len(B_CHUNKS)
    return pl.pallas_call(
        functools.partial(expert_kernel, groups, width),
        name="experts",
        out_shape=(
            jax.ShapeDtypeStruct((groups, 256, hidden), BF16),
            jax.ShapeDtypeStruct(tokens.shape, BF16),
            jax.ShapeDtypeStruct(router.shape, F32),
            jax.ShapeDtypeStruct((8, 128), F32),
        ),
        in_specs=[anywhere] * 5,
        out_specs=(anywhere, anywhere, anywhere, pl.BlockSpec(memory_space=pltpu.VMEM)),
        scratch_shapes=[
            pltpu.VMEM((NC, 2, groups, NZ, NX, ROWS, width), BF16),
            pltpu.VMEM((2, 4, hidden, width), BF16),
            pltpu.VMEM((groups, 256, hidden), F32),
            pltpu.VMEM((groups, 256, hidden), BF16),
            pltpu.VMEM((256, depth // 2), BF16),
            pltpu.VMEM((NZ, 2, 8, 128), F32),
            pltpu.VMEM((NZ, EXPERTS, groups * ROWS, 256), BF16),
            pltpu.VMEM((na, EXPERTS, groups, ROWS, width), BF16),
            pltpu.VMEM((nb, NZ, 256, width), BF16),
            pltpu.VMEM((nb, EXPERTS, groups, NZ, ROWS, width), BF16),
            pltpu.VMEM((EXPERTS, 8, 256), F32),
            pltpu.VMEM((NZ, NX, 8, 256), F32),
            pltpu.VMEM((8, 128), F32),
            pltpu.VMEM((16, 8, 256), F32),
            pltpu.VMEM((16, 8, 256), F32),
            pltpu.VMEM((2, EXPERTS, 8, 256), F32),
            pltpu.VMEM((2, 8, 128), F32),
            dma((2,)), dma((2, 4)), dma((groups,)), dma((groups,)), dma((NC + 2,)), dma((5,)), dma((5,)),
            dma((NC + 1, 3)), dma((NC + 1, 3)), dma((NC + 2, 3)), dma((NC + 2, 3)), dma((NC + 1, 4)), dma((NC + 1, 4)),
            dma((15,)), dma((15,)),
        ],
        compiler_params=pltpu.CompilerParams(
            collective_id=0, has_side_effects=True, vmem_limit_bytes=67043328
        ),
        cost_estimate=pl.CostEstimate(
            flops=2 * groups * 256 * depth * hidden, bytes_accessed=200_000_000, transcendentals=0
        ),
    )(tokens, info, saved, weight, router)


def last_kernel(grad_ref, tokens_ref, router_ref, spread_ref, hidden_ref, upstream_ref, perm):
    @pl.when(pl.program_id(0) == 0)
    def _():
        perm[...] = permutation(True)

    for g in range(grad_ref.shape[0]):
        hidden_ref[g] = jnp.dot(perm[...], grad_ref[g], preferred_element_type=F32).astype(BF16)
    live = lax.axis_index("section") < lax.axis_size("section") - 1
    spread = jnp.transpose(spread_ref[...])
    total = tokens_ref[...].astype(F32)
    for e in range(EXPERTS):
        total = total + spread[:, e : e + 1] * router_ref[e : e + 1, :]
    upstream_ref[...] = jnp.where(live, total, 0.0).astype(BF16)


def last_call(grad, tokens, router, spread):
    groups, rows, hidden = grad.shape
    flat, depth = tokens.shape
    steps = 3
    grad_spec = pl.BlockSpec((groups // steps, rows, hidden), lambda s: (s, 0, 0))
    token_spec = pl.BlockSpec((flat, depth // steps), lambda s: (0, s))
    return pl.pallas_call(
        last_kernel,
        name="last",
        grid=(steps,),
        out_shape=(jax.ShapeDtypeStruct(grad.shape, BF16), jax.ShapeDtypeStruct(tokens.shape, BF16)),
        in_specs=[
            grad_spec,
            token_spec,
            pl.BlockSpec((EXPERTS, depth // steps), lambda s: (0, s)),
            pl.BlockSpec((8, 128), lambda s: (0, 0)),
        ],
        out_specs=(grad_spec, token_spec),
        scratch_shapes=[pltpu.VMEM((256, 256), BF16)],
    )(grad, tokens, router, spread)


def local(upstream_dy, gate_logits, expert_ids, saved_hidden, down_weight, router_weight):
    micro, per, depth = upstream_dy.shape[1:]
    hidden = down_weight.shape[1]
    flat = micro * per
    info = jnp.concatenate(
        [
            expert_ids[0].transpose(2, 0, 1).reshape(2, flat).astype(F32),
            gate_logits[0].transpose(2, 0, 1).reshape(2, flat),
            jnp.zeros((4, flat), F32),
        ]
    )
    saved = saved_hidden[0].transpose(0, 2, 1, 3).reshape(micro * CAP // 8, 256, hidden)
    grad, tokens, router, spread = expert_call(
        upstream_dy[0].reshape(flat, depth), info, saved, down_weight[0], router_weight[0].T
    )
    hidden_grad, upstream = last_call(grad, tokens, router, spread)
    hidden_grad = hidden_grad.reshape(micro, CAP, NX * NZ * 2, hidden).transpose(0, 2, 1, 3)
    return (hidden_grad[None], upstream.reshape(micro, per, depth)[None])


def solution(mesh):
    placed = (
        P("section", None, "expert", None),
        P("section", None, "expert", None),
        P("section", None, "expert", None),
        P("section", None, None, None, "expert"),
        P("section", "expert", None),
        P("section", None, None),
    )
    return jax.shard_map(
        local,
        mesh=mesh,
        in_specs=placed,
        out_specs=(P("section", None, None, None, "expert"), P("section", None, "expert", None)),
        check_vma=False,
    )
```

```python
import functools

import jax
import jax.numpy as jnp
from jax import lax
from jax.experimental import pallas as pl
from jax.experimental.pallas import tpu as pltpu
from jax.sharding import PartitionSpec as P

EXPERTS = 4
CAP = 36
NX = 4
NZ = 4
NC = 12
A_CHUNKS = (0, 2, 4, 6, 8, 10, 11)
B_CHUNKS = (1, 3, 5, 7, 9)
ORDER = ((1, 0), (3, 2), (4, 5), (6, 7), (8,), (10,), (9,), (11,))
PIECES = 12
FIRST = (
    "t1", "g12", "x12", "p0", "p2", "x0", "t3", "t5", "p4", "x2", "t7", "p6",
    "x4", "p8", "x6", "t9", "p10", "x8", "p11", "x10", "x11",
)
EARLY = (
    "r1", "r3", "a0", "r5", "c1", "r7", "c3", "r9", "a2", "c5", "c7", "c9",
)
LATE = (
    "n0", "a4", "n2", "a6", "w1", "f0", "m0", "n4", "a8", "w3", "f2", "m1",
    "n6", "a10", "f4", "w5", "n8", "a11", "m2", "f6", "n10", "w7", "m3", "f8",
    "n11", "m4", "f10", "w9", "m5", "f11", "m6",
)
ROWS = 16
MESH = pl.DeviceIdType.MESH
F32 = jnp.float32
BF16 = jnp.bfloat16
NT = (((1,), (1,)), ((), ()))
HIGHEST = lax.Precision.HIGHEST


def permutation(turned):
    i = lax.broadcasted_iota(jnp.int32, (256, 256), 1 if turned else 0)
    n = lax.broadcasted_iota(jnp.int32, (256, 256), 0 if turned else 1)
    z, x, src, slot = i >> 6, (i >> 4) & 3, (i >> 3) & 1, i & 7
    return (n == slot * 32 + (x * 4 + z) * 2 + src).astype(F32).astype(BF16)


def codes_of(ids, logits, src):
    chosen = [jnp.concatenate([ids[0, k : k + 1], ids[1, k : k + 1]], axis=1) for k in range(2)]
    picks = [[(row == e).astype(F32) for e in range(EXPERTS)] for row in chosen]
    picked = jnp.concatenate([a + b for a, b in zip(*picks)] * 2, axis=0)
    t = lax.broadcasted_iota(jnp.int32, (128, 128), 0)
    u = lax.broadcasted_iota(jnp.int32, (128, 128), 1)
    earlier = ((t < u) & ((t >> 6) == (u >> 6))).astype(F32).astype(BF16)
    rank = jnp.dot(picked.astype(BF16), earlier, preferred_element_type=F32)
    micro = (lax.broadcasted_iota(jnp.int32, (8, 128), 1) >> 6).astype(F32)
    slot = rank + micro * CAP
    base = jnp.floor(slot * 0.125)
    code = jnp.where(picked > 0, base * 8 + slot + src * 8, -1.0)
    if logits is None:
        return code, None
    logit = [jnp.concatenate([logits[0, k : k + 1], logits[1, k : k + 1]], axis=1) for k in range(2)]
    diff = logit[0] - logit[1]
    first, second = jax.nn.sigmoid(diff), jax.nn.sigmoid(-diff)
    gate = jnp.concatenate([a * first + b * second for a, b in zip(*picks)] * 2, axis=0)
    return code, gate


def expert_kernel(
    groups, width, x_hbm, ids_hbm, logits_hbm, saved_hbm, w_hbm, router_hbm, grad_hbm, next_hbm, nrouter_hbm, spread_ref,
    rows, wv, acc, sv, x2, info, logits, selz, packed, raw_z, packed_z, gs, gt, own_gate, pts, pr, sums, spread,
    x_sem, w_sem, s_sem, o_sem, loc_sem, b0_send, b0_recv, xs, xr, zs, zr, bs, br, ps, pr_sem,
):
    me = lax.axis_index("expert")
    section = lax.axis_index("section")
    mx, mz, mc = me // 8, (me // 2) % 4, me % 2
    half = width * NC

    def dev(x, z, c, s=0):
        index = (lax.rem(x + 8, NX) * NZ + lax.rem(z + 8, NZ)) * 2 + c
        return (lax.rem(section + s + 4, 4), index)

    sibling = dev(mx, mz, 1 - mc)
    xdev = [dev(mx + d, mz, mc) for d in range(NX)]
    zdev = [dev(mx, mz + d, mc) for d in range(NZ)]
    before, after = dev(mx, mz, mc, -1), dev(mx, mz, mc, 1)
    chips = [(dx, dz) for dx in range(NX) for dz in range(NZ) if dx or dz]

    def remote(src, dst, send, recv, target):
        return pltpu.make_async_remote_copy(
            src_ref=src, dst_ref=dst, send_sem=send, recv_sem=recv, device_id=target, device_id_type=MESH
        )

    waits = []

    def send(src, dst, send_sem, recv_sem, target):
        copy = remote(src, dst, send_sem, recv_sem, target)
        copy.start()
        waits.append(copy)

    def arrived(ref, sem):
        remote(ref, ref, b0_send.at[0], sem, sibling).wait_recv()

    mine_rows = pl.ds(pl.multiple_of(mc * 128, 128), 128)
    sib_rows = pl.ds(pl.multiple_of((1 - mc) * 128, 128), 128)
    own_c = pltpu.make_async_copy(ids_hbm, info.at[mz, mc], x_sem.at[PIECES])
    own_c.start()
    own_l = pltpu.make_async_copy(logits_hbm, logits.at[mc], x_sem.at[PIECES + 1])
    own_l.start()
    piece = half // PIECES
    own_x = []
    for q in range(PIECES):
        cols = pl.ds(pl.multiple_of(mc * half + q * piece, 128), piece)
        own_x.append(
            pltpu.make_async_copy(x_hbm.at[:, cols], x2.at[mine_rows, q * piece : (q + 1) * piece], x_sem.at[q])
        )
        own_x[q].start()

    barrier = pltpu.get_barrier_semaphore()
    partners = [sibling, before, after] + [dev(mx + dx, mz + dz, mc) for dx, dz in chips]
    for target in partners:
        pl.semaphore_signal(barrier, inc=1, device_id=target, device_id_type=MESH)
    pl.semaphore_wait(barrier, len(partners))

    send(ids_hbm, info.at[mz, mc], b0_send.at[1], b0_recv.at[1], sibling)
    send(logits_hbm, logits.at[mc], b0_send.at[0], b0_recv.at[0], sibling)
    for q in range(PIECES):
        cols = pl.ds(pl.multiple_of((1 - mc) * half + q * piece, 128), piece)
        to = x2.at[mine_rows, q * piece : (q + 1) * piece]
        send(x_hbm.at[:, cols], to, b0_send.at[5 + q], b0_recv.at[5 + q], sibling)
    swapped = set()

    def swap_done(k):
        q = k * width // piece
        if q not in swapped:
            swapped.add(q)
            own_x[q].wait()
            arrived(x2.at[sib_rows, q * piece : (q + 1) * piece], b0_recv.at[5 + q])

    def w_copies(i):
        copies = []
        for n, k in enumerate(ORDER[i]):
            for h in range(2):
                cols = pl.ds(h * half + k * width, width)
                copies.append(
                    pltpu.make_async_copy(w_hbm.at[:, cols], wv.at[i % 2, n * 2 + h], w_sem.at[i % 2, n * 2 + h])
                )
        return copies

    for i in range(2):
        for copy in w_copies(i):
            copy.start()
    s_copy = [pltpu.make_async_copy(saved_hbm.at[g], sv.at[g], s_sem.at[g]) for g in range(groups)]
    for copy in s_copy:
        copy.start()
    send(x_hbm, next_hbm, b0_send.at[2], b0_recv.at[2], before)
    send(router_hbm, nrouter_hbm, b0_send.at[3], b0_recv.at[3], before)

    def select(z, own=False):
        code0, gate0 = codes_of(info[z, 0], logits[0] if own else None, 0)
        code1, gate1 = codes_of(info[z, 1], logits[1] if own else None, 1)
        row = lax.broadcasted_iota(jnp.int32, (groups * ROWS, 256), 0).astype(F32)
        gates = []
        for e in range(EXPERTS):
            code = jnp.concatenate([code0[e : e + 1], code1[e : e + 1]], axis=1)
            selz[z, e] = (row == code).astype(F32).astype(BF16)
            if own:
                gates.append(jnp.concatenate([gate0[e : e + 1], gate1[e : e + 1]], axis=1))
        return gates, gate0, gate1

    gs[...] = jnp.zeros_like(gs)

    def own_select(_):
        own_c.wait()
        own_l.wait()
        arrived(info.at[mz, 1 - mc], b0_recv.at[1])
        arrived(logits.at[1 - mc], b0_recv.at[0])
        for d in (1, 3, 2):
            send(info.at[mz], info.at[mz], zs.at[NC + 1, d - 1], zr.at[NC + 1, d - 1], zdev[d])
        gates, gate0, gate1 = select(mz, True)
        own_gate[...] = jnp.where(mc == 0, gate0, gate1)
        for e in range(EXPERTS):
            gs[e, :, 0 : groups * ROWS] = lax.dot_general(
                jnp.broadcast_to(gates[e], (8, 256)).astype(BF16), selz[mz, e], NT, preferred_element_type=F32
            )

    def columns(k):
        return slice(k * width, (k + 1) * width)

    def start_raw(k):
        b = B_CHUNKS.index(k)
        swap_done(k)
        for d in (1, 3):
            send(x2.at[:, columns(k)], raw_z.at[b, mz], zs.at[k, d - 1], zr.at[k, d - 1], zdev[d])

    def relay_raw(k):
        b = B_CHUNKS.index(k)
        for d, part in ((1, pl.ds(0, 128)), (3, pl.ds(128, 128))):
            z = lax.rem(mz - d + NZ, NZ)
            arrived(raw_z.at[b, z], zr.at[k, d - 1])
            ref = raw_z.at[b, z, part]
            send(ref, ref, zs.at[k, 1 if d == 1 else 3], zr.at[k, 1 if d == 1 else 3], zdev[d])

    def pack(k):
        a = A_CHUNKS.index(k)
        swap_done(k)
        for e in range(EXPERTS):
            block = jnp.dot(selz[mz, e], x2[:, columns(k)], preferred_element_type=F32)
            packed[a, e] = block.astype(BF16).reshape(groups, ROWS, width)

    locals_ = {}

    def start_x(k):
        if k == NC:
            here = gs.at
            there = gt.at[mz, mx]
        elif k in A_CHUNKS:
            here = packed.at[A_CHUNKS.index(k)].at
            there = rows.at[k, mc, :, mz, mx]
        else:
            here = packed_z.at[B_CHUNKS.index(k)].at
            there = rows.at[k, mc, :, :, mx]
        locals_[k] = pltpu.make_async_copy(here[mx], there, loc_sem.at[k])
        locals_[k].start()
        for d in (2, 1, 3):
            send(here[lax.rem(mx + d, NX)], there, xs.at[k, d - 1], xr.at[k, d - 1], xdev[d])

    def wait_x(k):
        locals_[k].wait()
        for d in (1, 2, 3):
            x = lax.rem(mx - d + NX, NX)
            if k == NC:
                ref = gt.at[mz, x]
            elif k in A_CHUNKS:
                ref = rows.at[k, mc, :, mz, x]
            else:
                ref = rows.at[k, mc, :, :, x]
            arrived(ref, xr.at[k, d - 1])

    def around_z(k):
        wait_x(k)
        ref = gt.at[mz] if k == NC else rows.at[k, mc, :, mz]
        for d in (1, 3, 2) if k == NC else (1, 3):
            send(ref, ref, zs.at[k, d - 1], zr.at[k, d - 1], zdev[d])
        if k < NC:
            send(ref, ref, bs.at[k, 0], br.at[k, 0], sibling)

    def cross_x(k):
        b = B_CHUNKS.index(k)
        opposite = lax.rem(mz + 2, NZ)
        arrived(raw_z.at[b, opposite, pl.ds(0, 128)], zr.at[k, 1])
        arrived(raw_z.at[b, opposite, pl.ds(128, 128)], zr.at[k, 3])
        for d in range(NZ):
            z = lax.rem(mz + d, NZ)
            tokens = raw_z[b, z] if d else x2[:, columns(k)]
            for e in range(EXPERTS):
                block = jnp.dot(selz[z, e], tokens, preferred_element_type=F32)
                packed_z[b, e, :, z] = block.astype(BF16).reshape(groups, ROWS, width)
        start_x(k)

    def near(k):
        for d, part in ((1, pl.ds(0, 2)), (3, pl.ds(2, 2))):
            z = lax.rem(mz - d + NZ, NZ)
            ref = rows.at[k, mc, :, z]
            arrived(ref, zr.at[k, d - 1])
            ref = rows.at[k, mc, :, z, part]
            send(ref, ref, zs.at[k, 1 if d == 1 else 3], zr.at[k, 1 if d == 1 else 3], zdev[d])
            ref = rows.at[k, mc, :, z]
            send(ref, ref, bs.at[k, d], br.at[k, d], sibling)

    def far(k):
        opposite = lax.rem(mz + 2, NZ)
        arrived(rows.at[k, mc, :, opposite, pl.ds(0, 2)], zr.at[k, 1])
        arrived(rows.at[k, mc, :, opposite, pl.ds(2, 2)], zr.at[k, 3])
        ref = rows.at[k, mc, :, opposite]
        send(ref, ref, bs.at[k, 2], br.at[k, 2], sibling)

    def whole(k):
        wait_x(k)
        send(rows.at[k, mc], rows.at[k, mc], bs.at[k, 0], br.at[k, 0], sibling)

    def shared(k):
        if k in A_CHUNKS:
            for d in range(NZ):
                arrived(rows.at[k, 1 - mc, :, lax.rem(mz - d + NZ, NZ)], br.at[k, d])
        else:
            arrived(rows.at[k, 1 - mc], br.at[k, 0])

    big = groups // 3

    def compute(i):
        for k in ORDER[i]:
            shared(k)
        for copy in w_copies(i):
            copy.wait()

        def body(m, carry):
            at = pl.ds(m * big, big)
            total = None
            for n, k in enumerate(ORDER[i]):
                for h in range(2):
                    left = rows[k, h, at].reshape(big * 256, width)
                    term = lax.dot_general(left, wv[i % 2, n * 2 + h], NT, preferred_element_type=F32)
                    total = term if total is None else total + term
            total = total.reshape(big, 256, total.shape[-1])
            acc[at] = total if i == 0 else acc[at] + total
            return carry

        lax.fori_loop(0, 3, body, 0)
        if i + 2 < len(ORDER):
            for copy in w_copies(i + 2):
                copy.start()

    def in_order(names):
        steps = {
            "t": start_raw, "r": relay_raw, "c": cross_x, "g": own_select, "p": pack, "x": start_x, "a": around_z,
            "n": near, "f": far, "w": whole, "m": compute,
        }
        for word in names:
            steps[word[0]](int(word[1:]))

    in_order(FIRST)
    around_z(NC)
    for d in (1, 2, 3):
        z = lax.rem(mz + d, NZ)
        arrived(info.at[z], zr.at[NC + 1, NZ - d - 1])
        select(z)
    in_order(EARLY)
    perm = permutation(False)

    def place_saved(g, carry):
        sv[g] = jnp.dot(perm, sv[g], preferred_element_type=F32).astype(BF16)
        return carry

    for copy in s_copy:
        copy.wait()
    lax.fori_loop(0, groups, place_saved, 0)
    for d in (1, 2, 3):
        arrived(gt.at[lax.rem(mz - d + NZ, NZ)], zr.at[NC, d - 1])
    in_order(LATE)
    (k,) = ORDER[-1]
    last = (len(ORDER) - 1) % 2
    for copy in w_copies(len(ORDER) - 1):
        copy.wait()

    def term_of(at, h):
        left = rows[k, h, at].reshape(big * 256, width)
        term = lax.dot_general(left, wv[last, h], NT, preferred_element_type=F32)
        return acc[at] + term.reshape(big, 256, term.shape[-1])

    def own_half(m, carry):
        at = pl.ds(m * big, big)
        acc[at] = term_of(at, mc)
        return carry

    lax.fori_loop(0, 3, own_half, 0)
    shared(k)

    lane = lax.broadcasted_iota(jnp.int32, (256, 256), 1)
    row16 = lax.broadcasted_iota(jnp.int32, (256, 256), 0) & 15

    def dots(m, total):
        at = pl.ds(m * big, big)
        raw = term_of(at, 1 - mc)
        acc[at] = raw
        part = jnp.sum(raw * sv[at].astype(F32), axis=2, keepdims=True)
        for n in range(big):
            placed = jnp.where(lane == row16 + (m * big + n) * 16, part[n], 0.0)
            total = total + jnp.sum(placed.reshape(16, 16, 256), axis=1)
        return total

    part = lax.fori_loop(0, 3, dots, jnp.zeros((16, 256), F32))
    pts[...] = jnp.broadcast_to(part[:, None, :], (16, 8, 256))
    slot = mx * NZ + mz
    own_part = pltpu.make_async_copy(pts.at[mz * NX + mx], pr.at[slot], loc_sem.at[NC + 1])
    own_part.start()
    for n, (dx, dz) in enumerate(chips):
        x, z = lax.rem(mx + dx, NX), lax.rem(mz + dz, NZ)
        send(pts.at[z * NX + x], pr.at[slot], ps.at[n], pr_sem.at[n], dev(x, z, mc))

    gates = jnp.broadcast_to(gt[...].reshape(16, 8, 256)[:, 0:1, :], (16, 16, 256)).reshape(256, 256)

    back = permutation(True)

    def finish(g, carry):
        gate = jnp.sum(jnp.where(lane == row16 + g * 16, gates, 0.0), axis=1, keepdims=True)
        grad = (gate * acc[g]).astype(BF16)
        sv[g] = jnp.dot(back, grad, preferred_element_type=F32).astype(BF16)
        pltpu.make_async_copy(sv.at[g], grad_hbm.at[g], o_sem.at[g]).start()
        return carry

    lax.fori_loop(0, groups, finish, 0)

    own_part.wait()
    for n, (dx, dz) in enumerate(chips):
        x, z = lax.rem(mx - dx + NX, NX), lax.rem(mz - dz + NZ, NZ)
        arrived(pr.at[x * NZ + z], pr_sem.at[n])
    summed = jnp.sum(pr[...].reshape(EXPERTS, NZ, 8, 256), axis=1)
    sums[0] = summed
    send(sums.at[0], sums.at[1], bs.at[NC, 0], br.at[NC, 0], sibling)
    arrived(sums.at[1], br.at[NC, 0])
    summed = summed + sums[1]
    token = []
    for e in range(EXPERTS):
        chosen = jnp.where(mc == 0, selz[mz, e, :, 0:128].astype(F32), selz[mz, e, :, 128:256].astype(F32))
        token.append(
            jnp.dot(summed[e, :, 0 : groups * ROWS], chosen, preferred_element_type=F32, precision=HIGHEST)[0:1]
        )
    token = jnp.concatenate(token * 2, axis=0)
    gate = own_gate[...]
    mixed = jnp.sum((gate * token)[0:EXPERTS], axis=0, keepdims=True)
    spread[0] = gate * (token - mixed)
    send(spread.at[0], spread.at[1], b0_send.at[4], b0_recv.at[4], before)
    for g in range(groups):
        pltpu.make_async_copy(sv.at[g], grad_hbm.at[g], o_sem.at[g]).wait()
    arrived(next_hbm, b0_recv.at[2])
    arrived(nrouter_hbm, b0_recv.at[3])
    arrived(spread.at[1], b0_recv.at[4])
    spread_ref[...] = spread[1]
    for copy in waits:
        copy.wait_send()


def expert_call(tokens, ids, logits, saved, weight, router):
    depth, hidden = tokens.shape[-1], weight.shape[0]
    groups = saved.shape[0]
    width = depth // 2 // NC
    dma = pltpu.SemaphoreType.DMA
    anywhere = pl.BlockSpec(memory_space=pl.ANY)
    na, nb = len(A_CHUNKS), len(B_CHUNKS)
    return pl.pallas_call(
        functools.partial(expert_kernel, groups, width),
        name="experts",
        out_shape=(
            jax.ShapeDtypeStruct((groups, 256, hidden), BF16),
            jax.ShapeDtypeStruct(tokens.shape, BF16),
            jax.ShapeDtypeStruct(router.shape, F32),
            jax.ShapeDtypeStruct((8, 128), F32),
        ),
        in_specs=[anywhere] * 6,
        out_specs=(anywhere, anywhere, anywhere, pl.BlockSpec(memory_space=pltpu.VMEM)),
        scratch_shapes=[
            pltpu.VMEM((NC, 2, groups, NZ, NX, ROWS, width), BF16),
            pltpu.VMEM((2, 4, hidden, width), BF16),
            pltpu.VMEM((groups, 256, hidden), F32),
            pltpu.VMEM((groups, 256, hidden), BF16),
            pltpu.VMEM((256, depth // 2), BF16),
            pltpu.VMEM((NZ, 2) + ids.shape, jnp.int32),
            pltpu.VMEM((2,) + ids.shape, F32),
            pltpu.VMEM((NZ, EXPERTS, groups * ROWS, 256), BF16),
            pltpu.VMEM((na, EXPERTS, groups, ROWS, width), BF16),
            pltpu.VMEM((nb, NZ, 256, width), BF16),
            pltpu.VMEM((nb, EXPERTS, groups, NZ, ROWS, width), BF16),
            pltpu.VMEM((EXPERTS, 8, 256), F32),
            pltpu.VMEM((NZ, NX, 8, 256), F32),
            pltpu.VMEM((8, 128), F32),
            pltpu.VMEM((16, 8, 256), F32),
            pltpu.VMEM((16, 8, 256), F32),
            pltpu.VMEM((2, EXPERTS, 8, 256), F32),
            pltpu.VMEM((2, 8, 128), F32),
            dma((PIECES + 2,)), dma((2, 4)), dma((groups,)), dma((groups,)), dma((NC + 2,)), dma((5 + PIECES,)), dma((5 + PIECES,)),
            dma((NC + 1, 3)), dma((NC + 1, 3)), dma((NC + 2, 4)), dma((NC + 2, 4)), dma((NC + 1, 4)), dma((NC + 1, 4)),
            dma((15,)), dma((15,)),
        ],
        compiler_params=pltpu.CompilerParams(
            collective_id=0, has_side_effects=True, vmem_limit_bytes=67043328
        ),
        cost_estimate=pl.CostEstimate(
            flops=2 * groups * 256 * depth * hidden, bytes_accessed=200_000_000, transcendentals=0
        ),
    )(tokens, ids, logits, saved, weight, router)


def last_kernel(
    grad_hbm, tokens_hbm, router_ref, spread_ref, hidden_hbm, upstream_hbm,
    grad, tokens, upstream, grad_in, grad_out, token_in, token_out,
):
    groups, pieces = grad.shape[0], tokens.shape[0]
    width = tokens.shape[2]
    reads, token_reads, writes = [], [], []
    for q in range(pieces):
        cols = pl.ds(q * width, width)
        token_reads.append(pltpu.make_async_copy(tokens_hbm.at[:, cols], tokens.at[q], token_in.at[q]))
        token_reads[q].start()
    for g in range(groups):
        reads.append(pltpu.make_async_copy(grad_hbm.at[g], grad.at[g], grad_in.at[g]))
        reads[g].start()

    def write(src, dst, sem):
        writes.append(pltpu.make_async_copy(src, dst, sem))
        writes[-1].start()

    live = lax.axis_index("section") < lax.axis_size("section") - 1
    spread = jnp.transpose(spread_ref[...])
    for q in range(pieces):
        token_reads[q].wait()
        total = tokens[q].astype(F32)
        for e in range(EXPERTS):
            total = total + spread[:, e : e + 1] * router_ref[e : e + 1, q * width : (q + 1) * width]
        upstream[q] = jnp.where(live, total, 0.0).astype(BF16)
        write(upstream.at[q], upstream_hbm.at[:, pl.ds(q * width, width)], token_out.at[q])
        for g in range(q * groups // pieces, (q + 1) * groups // pieces):
            reads[g].wait()
            write(grad.at[g], hidden_hbm.at[g], grad_out.at[g])
    for copy in writes:
        copy.wait()


def last_call(grad, tokens, router, spread):
    groups = grad.shape[0]
    flat, depth = tokens.shape
    pieces = 4
    anywhere = pl.BlockSpec(memory_space=pl.ANY)
    whole = pl.BlockSpec(memory_space=pltpu.VMEM)
    dma = pltpu.SemaphoreType.DMA
    return pl.pallas_call(
        last_kernel,
        name="last",
        out_shape=(jax.ShapeDtypeStruct(grad.shape, BF16), jax.ShapeDtypeStruct(tokens.shape, BF16)),
        in_specs=[anywhere, anywhere, whole, whole],
        out_specs=(anywhere, anywhere),
        scratch_shapes=[
            pltpu.VMEM(grad.shape, BF16),
            pltpu.VMEM((pieces, flat, depth // pieces), BF16),
            pltpu.VMEM((pieces, flat, depth // pieces), BF16),
            dma((groups,)), dma((groups,)), dma((pieces,)), dma((pieces,)),
        ],
        compiler_params=pltpu.CompilerParams(vmem_limit_bytes=67043328),
    )(grad, tokens, router, spread)


def local(upstream_dy, gate_logits, expert_ids, saved_hidden, down_weight, router_weight):
    micro, per, depth = upstream_dy.shape[1:]
    hidden = down_weight.shape[1]
    flat = micro * per
    saved = saved_hidden[0].transpose(0, 2, 1, 3).reshape(micro * CAP // 8, 256, hidden)
    grad, tokens, router, spread = expert_call(
        upstream_dy[0].reshape(flat, depth), expert_ids[0].transpose(0, 2, 1), gate_logits[0].transpose(0, 2, 1), saved, down_weight[0], router_weight[0].T
    )
    hidden_grad, upstream = last_call(grad, tokens, router, spread)
    hidden_grad = hidden_grad.reshape(micro, CAP, NX * NZ * 2, hidden).transpose(0, 2, 1, 3)
    return (hidden_grad[None], upstream.reshape(micro, per, depth)[None])


def solution(mesh):
    placed = (
        P("section", None, "expert", None),
        P("section", None, "expert", None),
        P("section", None, "expert", None),
        P("section", None, None, None, "expert"),
        P("section", "expert", None),
        P("section", None, None),
    )
    return jax.shard_map(
        local,
        mesh=mesh,
        in_specs=placed,
        out_specs=(P("section", None, None, None, "expert"), P("section", None, "expert", None)),
        check_vma=False,
    )
```

```python
import functools

import jax
import jax.numpy as jnp
from jax import lax
from jax.experimental import pallas as pl
from jax.experimental.pallas import tpu as pltpu
from jax.sharding import PartitionSpec as P

EXPERTS = 4
CAP = 36
NX = 4
NZ = 4
NC = 12
A_CHUNKS = (0, 2, 4, 6, 8, 10, 11)
B_CHUNKS = (1, 3, 5, 7, 9)
PASSES = ((1, 0), (3, 2), (4, 5), (6,), (7,), (8,), (10,))
ORDER = (1, 0, 3, 2, 4, 5, 6, 7, 8, 10, 9, 11)
THIRDS = 9
HELD = 6
PIECES = 4
FIRST = (
    "t1", "g12", "x12", "p0", "p2", "x0", "t3", "t5", "p4", "x2", "t7", "p6",
    "x4", "p8", "x6", "t9", "p10", "x8", "p11", "x10", "x11",
)
EARLY = (
    "r1", "r3", "a0", "r5", "c1", "r7", "c3", "r9", "a2", "c5", "c7", "c9",
)
LATE = (
    "n0", "s0", "a4", "w101", "w201", "n2", "a6", "w301", "s2", "f0", "m0", "n4",
    "a8", "w103", "w203", "s4", "w303", "f2", "m1", "n6", "a10", "w105", "w205", "f4",
    "s6", "w305", "n8", "m2", "w107", "f6", "s8", "w207", "m3", "n10", "a11", "w307",
    "s10", "m4", "f8", "f10", "w109", "m5", "w209", "m109", "n11", "s11", "m6", "w309",
    "m209", "f11", "m309",
)
ROWS = 16
MESH = pl.DeviceIdType.MESH
F32 = jnp.float32
BF16 = jnp.bfloat16
NT = (((1,), (1,)), ((), ()))
HIGHEST = lax.Precision.HIGHEST


def permutation(turned):
    i = lax.broadcasted_iota(jnp.int32, (256, 256), 1 if turned else 0)
    n = lax.broadcasted_iota(jnp.int32, (256, 256), 0 if turned else 1)
    z, x, src, slot = i >> 6, (i >> 4) & 3, (i >> 3) & 1, i & 7
    return (n == slot * 32 + (x * 4 + z) * 2 + src).astype(F32).astype(BF16)


def codes_of(ids, logits, src):
    chosen = [jnp.concatenate([ids[0, k : k + 1], ids[1, k : k + 1]], axis=1) for k in range(2)]
    picks = [[(row == e).astype(F32) for e in range(EXPERTS)] for row in chosen]
    picked = jnp.concatenate([a + b for a, b in zip(*picks)] * 2, axis=0)
    t = lax.broadcasted_iota(jnp.int32, (128, 128), 0)
    u = lax.broadcasted_iota(jnp.int32, (128, 128), 1)
    earlier = ((t < u) & ((t >> 6) == (u >> 6))).astype(F32).astype(BF16)
    rank = jnp.dot(picked.astype(BF16), earlier, preferred_element_type=F32)
    micro = (lax.broadcasted_iota(jnp.int32, (8, 128), 1) >> 6).astype(F32)
    slot = rank + micro * CAP
    base = jnp.floor(slot * 0.125)
    code = jnp.where(picked > 0, base * 8 + slot + src * 8, -1.0)
    if logits is None:
        return code, None
    logit = [jnp.concatenate([logits[0, k : k + 1], logits[1, k : k + 1]], axis=1) for k in range(2)]
    diff = logit[0] - logit[1]
    first, second = jax.nn.sigmoid(diff), jax.nn.sigmoid(-diff)
    gate = jnp.concatenate([a * first + b * second for a, b in zip(*picks)] * 2, axis=0)
    return code, gate


def expert_kernel(
    groups, width, x_hbm, ids_hbm, logits_hbm, saved_hbm, w_hbm, router_hbm, grad_hbm, next_hbm, nrouter_hbm, spread_ref,
    rows, wv, acc, sv, x2, info, logits, selz, packed, raw_z, packed_z, gs, gt, next_gate, next_sel, next_ids, next_logits, pts, pr, sums, next_sums,
    x_sem, w_sem, s_sem, o_sem, loc_sem, sent, b0_recv, xa, xb, zr, br, pr_sem, next_sem,
):
    me = lax.axis_index("expert")
    section = lax.axis_index("section")
    mx, mz, mc = me // 8, (me // 2) % 4, me % 2
    half = width * NC

    def dev(x, z, c, s=0):
        index = (lax.rem(x + 8, NX) * NZ + lax.rem(z + 8, NZ)) * 2 + c
        return (lax.rem(section + s + 4, 4), index)

    sibling = dev(mx, mz, 1 - mc)
    xdev = [dev(mx + d, mz, mc) for d in range(NX)]
    zdev = [dev(mx, mz + d, mc) for d in range(NZ)]
    before, after = dev(mx, mz, mc, -1), dev(mx, mz, mc, 1)
    before_other, after_other = dev(mx, mz, 1 - mc, -1), dev(mx, mz, 1 - mc, 1)
    chips = [(dx, dz) for dx in range(NX) for dz in range(NZ) if dx or dz]

    def remote(src, dst, send, recv, target):
        return pltpu.make_async_remote_copy(
            src_ref=src, dst_ref=dst, send_sem=send, recv_sem=recv, device_id=target, device_id_type=MESH
        )

    def send(src, dst, recv_sem, target, kind):
        remote(src, dst, sent.at[kind], recv_sem, target).start()

    def drain(ref, kind):
        remote(ref, ref, sent.at[kind], b0_recv.at[0], sibling).wait_send()

    def arrived(ref, sem):
        remote(ref, ref, sent.at[0], sem, sibling).wait_recv()

    mine_rows = pl.ds(pl.multiple_of(mc * 128, 128), 128)
    sib_rows = pl.ds(pl.multiple_of((1 - mc) * 128, 128), 128)
    own_c = pltpu.make_async_copy(ids_hbm, info.at[mz, mc], x_sem.at[PIECES])
    own_c.start()
    own_l = pltpu.make_async_copy(logits_hbm, logits.at[mc], x_sem.at[PIECES + 1])
    own_l.start()
    piece = half // PIECES
    own_x = []
    for q in range(PIECES):
        cols = pl.ds(pl.multiple_of(mc * half + q * piece, 128), piece)
        own_x.append(
            pltpu.make_async_copy(x_hbm.at[:, cols], x2.at[mine_rows, q * piece : (q + 1) * piece], x_sem.at[q])
        )
        own_x[q].start()

    barrier = pltpu.get_barrier_semaphore()
    partners = [sibling, before, after, before_other, after_other] + [dev(mx + dx, mz + dz, mc) for dx, dz in chips]
    for target in partners:
        pl.semaphore_signal(barrier, inc=1, device_id=target, device_id_type=MESH)
    pl.semaphore_wait(barrier, len(partners))

    send(ids_hbm, info.at[mz, mc], b0_recv.at[1], sibling, 10)
    send(logits_hbm, logits.at[mc], b0_recv.at[0], sibling, 11)
    for q in range(PIECES):
        cols = pl.ds(pl.multiple_of((1 - mc) * half + q * piece, 128), piece)
        to = x2.at[mine_rows, q * piece : (q + 1) * piece]
        send(x_hbm.at[:, cols], to, b0_recv.at[6 + q], sibling, 8)
    swapped = set()

    def swap_done(k):
        q = k * width // piece
        if q not in swapped:
            swapped.add(q)
            own_x[q].wait()
            arrived(x2.at[sib_rows, q * piece : (q + 1) * piece], b0_recv.at[6 + q])

    def w_copies(k):
        slot = ORDER.index(k) % HELD
        copies = []
        for h in range(2):
            cols = pl.ds(h * half + k * width, width)
            copies.append(pltpu.make_async_copy(w_hbm.at[:, cols], wv.at[slot, h], w_sem.at[slot]))
        return copies

    for k in ORDER[:HELD]:
        for copy in w_copies(k):
            copy.start()
    s_copy = [pltpu.make_async_copy(saved_hbm, sv, s_sem.at[0])]
    s_copy[0].start()
    send(ids_hbm, next_ids, b0_recv.at[4], before, 15)
    send(logits_hbm, next_logits, b0_recv.at[5], before, 14)
    send(x_hbm, next_hbm, b0_recv.at[2], before, 12)
    send(router_hbm, nrouter_hbm, b0_recv.at[3], before, 13)

    def select(z, own=False):
        code0, gate0 = codes_of(info[z, 0], logits[0] if own else None, 0)
        code1, gate1 = codes_of(info[z, 1], logits[1] if own else None, 1)
        row = lax.broadcasted_iota(jnp.int32, (groups * ROWS, 256), 0).astype(F32)
        gates = []
        for e in range(EXPERTS):
            code = jnp.concatenate([code0[e : e + 1], code1[e : e + 1]], axis=1)
            selz[z, e] = (row == code).astype(F32).astype(BF16)
            if own:
                gates.append(jnp.concatenate([gate0[e : e + 1], gate1[e : e + 1]], axis=1))
        return gates

    gs[...] = jnp.zeros_like(gs)

    def own_select(_):
        own_c.wait()
        own_l.wait()
        arrived(info.at[mz, 1 - mc], b0_recv.at[1])
        arrived(logits.at[1 - mc], b0_recv.at[0])
        for d in (1, 3, 2):
            send(info.at[mz], info.at[mz], zr.at[NC + 1, d - 1], zdev[d], 5)
        gates = select(mz, True)
        for e in range(EXPERTS):
            gs[e, :, 0 : groups * ROWS] = lax.dot_general(
                jnp.broadcast_to(gates[e], (8, 256)).astype(BF16), selz[mz, e], NT, preferred_element_type=F32
            )

    def columns(k):
        return slice(k * width, (k + 1) * width)

    third = groups // 3

    parts = [pl.ds(p * third, third) for p in range(3)]

    def start_raw(k):
        b = B_CHUNKS.index(k)
        swap_done(k)
        for d in (1, 3):
            send(x2.at[:, columns(k)], raw_z.at[b, mz], zr.at[k, d - 1], zdev[d], 3)

    def relay_raw(k):
        b = B_CHUNKS.index(k)
        for d, part in ((1, pl.ds(0, 128)), (3, pl.ds(128, 128))):
            z = lax.rem(mz - d + NZ, NZ)
            arrived(raw_z.at[b, z], zr.at[k, d - 1])
            ref = raw_z.at[b, z, part]
            send(ref, ref, zr.at[k, 1], zdev[d], 3)

    def pack(k):
        a = A_CHUNKS.index(k)
        swap_done(k)
        for e in range(EXPERTS):
            block = jnp.dot(selz[mz, e], x2[:, columns(k)], preferred_element_type=F32)
            packed[a, e] = block.astype(BF16).reshape(groups, ROWS, width)

    locals_ = {}

    def start_x(k):
        if k == NC:
            locals_[k] = pltpu.make_async_copy(gs.at[mx], gt.at[mz, mx], loc_sem.at[k])
        elif k in A_CHUNKS:
            locals_[k] = pltpu.make_async_copy(
                packed.at[A_CHUNKS.index(k), mx], rows.at[k, mc, :, mz, mx], loc_sem.at[k]
            )
        else:
            locals_[k] = pltpu.make_async_copy(
                packed_z.at[B_CHUNKS.index(k), mx], rows.at[k, mc, :, :, mx], loc_sem.at[k]
            )
        locals_[k].start()
        for p, at in enumerate(parts if k in B_CHUNKS else parts[:1]):
            for d in (2, 1, 3):
                e = lax.rem(mx + d, NX)
                if k == NC:
                    send(gs.at[e], gt.at[mz, mx], xa.at[len(A_CHUNKS), d - 1], xdev[d], 6)
                elif k in A_CHUNKS:
                    a = A_CHUNKS.index(k)
                    send(packed.at[a, e], rows.at[k, mc, :, mz, mx], xa.at[a, d - 1], xdev[d], 0)
                else:
                    b = B_CHUNKS.index(k)
                    send(packed_z.at[b, e, at], rows.at[k, mc, at, :, mx], xb.at[b, d - 1, p], xdev[d], 1)

    def around_z(k):
        locals_[k].wait()
        for d in (1, 2, 3):
            x = lax.rem(mx - d + NX, NX)
            a = len(A_CHUNKS) if k == NC else A_CHUNKS.index(k)
            arrived(gt.at[mz, x] if k == NC else rows.at[k, mc, :, mz, x], xa.at[a, d - 1])
        if k == NC:
            for d in (1, 3, 2):
                send(gt.at[mz], gt.at[mz], zr.at[k, d - 1], zdev[d], 7)
            return
        ref = rows.at[k, mc, :, mz]
        for d in (1, 3):
            send(ref, ref, zr.at[k, d - 1], zdev[d], 2)
        send(ref, ref, br.at[k, 0], sibling, 4)

    def cross_x(k):
        b = B_CHUNKS.index(k)
        opposite = lax.rem(mz + 2, NZ)
        arrived(raw_z.at[b, opposite], zr.at[k, 1])
        for d in range(NZ):
            z = lax.rem(mz + d, NZ)
            tokens = raw_z[b, z] if d else x2[:, columns(k)]
            for e in range(EXPERTS):
                block = jnp.dot(selz[z, e], tokens, preferred_element_type=F32)
                packed_z[b, e, :, z] = block.astype(BF16).reshape(groups, ROWS, width)
        start_x(k)

    def near(k):
        for d, share in ((1, pl.ds(0, 2)), (3, pl.ds(2, 2))):
            z = lax.rem(mz - d + NZ, NZ)
            arrived(rows.at[k, mc, :, z], zr.at[k, d - 1])
            ref = rows.at[k, mc, :, z, share]
            send(ref, ref, zr.at[k, 1], zdev[d], 2)

    def near_shared(k):
        for d in (1, 3):
            ref = rows.at[k, mc, :, lax.rem(mz - d + NZ, NZ)]
            send(ref, ref, br.at[k, 0], sibling, 4)

    def far(k):
        ref = rows.at[k, mc, :, lax.rem(mz + 2, NZ)]
        arrived(ref, zr.at[k, 1])
        send(ref, ref, br.at[k, 0], sibling, 4)

    def whole(step):
        k, p = step % 100, step // 100 - 1
        b, at = B_CHUNKS.index(k), parts[p]
        if p == 0:
            locals_[k].wait()
        for d in (1, 2, 3):
            arrived(rows.at[k, mc, at, :, lax.rem(mx - d + NX, NX)], xb.at[b, d - 1, p])
        send(rows.at[k, mc, at], rows.at[k, mc, at], br.at[k, p if k == THIRDS else 0], sibling, 4)

    def shared(k):
        arrived(rows.at[k, 1 - mc], br.at[k, 0])

    def terms(ks, at):
        total = None
        for k in ks:
            slot = ORDER.index(k) % HELD
            for h in range(2):
                left = rows[k, h, at].reshape(third * 256, width)
                term = lax.dot_general(left, wv[slot, h], NT, preferred_element_type=F32)
                total = term if total is None else total + term
        return total.reshape(third, 256, total.shape[-1])

    def w_ready(k):
        slot = ORDER.index(k) % HELD
        pltpu.make_async_copy(wv.at[slot], wv.at[slot], w_sem.at[slot]).wait()

    def compute(step):
        if step >= 100:
            k, p = step % 100, step // 100 - 1
            arrived(rows.at[k, 1 - mc, parts[p]], br.at[k, p])
            if p == 0:
                w_ready(k)
            acc[parts[p]] += terms((k,), parts[p])
            return
        ks = PASSES[step]
        for k in ks:
            shared(k)
            w_ready(k)

        def body(m, carry):
            at = pl.ds(m * third, third)
            total = terms(ks, at)
            acc[at] = total if step == 0 else acc[at] + total
            return carry

        lax.fori_loop(0, 3, body, 0)
        for k in ks:
            later = ORDER.index(k) + HELD
            if later < len(ORDER):
                for copy in w_copies(ORDER[later]):
                    copy.start()

    def in_order(names):
        steps = {
            "t": start_raw, "r": relay_raw, "c": cross_x, "g": own_select, "p": pack, "x": start_x, "a": around_z,
            "n": near, "f": far, "w": whole, "m": compute, "s": near_shared,
        }
        for word in names:
            steps[word[0]](int(word[1:]))

    in_order(FIRST)
    around_z(NC)
    for d in (1, 2, 3):
        z = lax.rem(mz + d, NZ)
        arrived(info.at[z], zr.at[NC + 1, NZ - d - 1])
        select(z)
    in_order(EARLY)
    perm = permutation(False)

    def place_saved(g, carry):
        sv[g] = jnp.dot(perm, sv[g], preferred_element_type=F32).astype(BF16)
        return carry

    arrived(next_ids, b0_recv.at[4])
    arrived(next_logits, b0_recv.at[5])
    code, gate = codes_of(next_ids, next_logits, mc.astype(F32))
    next_gate[...] = gate
    row = lax.broadcasted_iota(jnp.int32, (groups * ROWS, 128), 0).astype(F32)
    for e in range(EXPERTS):
        next_sel[e] = (row == code[e : e + 1]).astype(F32)
    for copy in s_copy:
        copy.wait()
    lax.fori_loop(0, groups, place_saved, 0)
    for d in (1, 2, 3):
        arrived(gt.at[lax.rem(mz - d + NZ, NZ)], zr.at[NC, d - 1])
    in_order(LATE)
    lane = lax.broadcasted_iota(jnp.int32, (256, 256), 1)
    row16 = lax.broadcasted_iota(jnp.int32, (256, 256), 0) & 15

    shared(ORDER[-1])
    w_ready(ORDER[-1])

    def dots(m, total):
        at = pl.ds(m * third, third)
        raw = acc[at] + terms(ORDER[-1:], at)
        acc[at] = raw
        part = jnp.sum(raw * sv[at].astype(F32), axis=2, keepdims=True)
        for n in range(third):
            placed = jnp.where(lane == row16 + (m * third + n) * 16, part[n], 0.0)
            total = total + jnp.sum(placed.reshape(16, 16, 256), axis=1)
        return total

    part = lax.fori_loop(0, 3, dots, jnp.zeros((16, 256), F32))
    pts[...] = jnp.broadcast_to(part[:, None, :], (16, 8, 256))
    slot = mx * NZ + mz
    own_part = pltpu.make_async_copy(pts.at[mz * NX + mx], pr.at[slot], loc_sem.at[NC + 1])
    own_part.start()
    for n, (dx, dz) in enumerate(chips):
        x, z = lax.rem(mx + dx, NX), lax.rem(mz + dz, NZ)
        send(pts.at[z * NX + x], pr.at[slot], pr_sem.at[n], dev(x, z, mc), 9)

    gates = jnp.broadcast_to(gt[...].reshape(16, 8, 256)[:, 0:1, :], (16, 16, 256)).reshape(256, 256)

    back = permutation(True)

    def finish(g, carry):
        gate = jnp.sum(jnp.where(lane == row16 + g * 16, gates, 0.0), axis=1, keepdims=True)
        grad = (gate * acc[g]).astype(BF16)
        sv[g] = jnp.dot(back, grad, preferred_element_type=F32).astype(BF16)
        pltpu.make_async_copy(sv.at[g], grad_hbm.at[g], o_sem.at[0]).start()
        return carry

    lax.fori_loop(0, groups, finish, 0)

    own_part.wait()
    for n, (dx, dz) in enumerate(chips):
        x, z = lax.rem(mx - dx + NX, NX), lax.rem(mz - dz + NZ, NZ)
        arrived(pr.at[x * NZ + z], pr_sem.at[n])
    summed = jnp.sum(pr[...].reshape(EXPERTS, NZ, 8, 256), axis=1)
    sums[...] = summed
    send(sums, next_sums.at[mc], next_sem.at[mc], before, 16)
    send(sums, next_sums.at[mc], next_sem.at[mc], before_other, 16)
    pltpu.make_async_copy(sv, grad_hbm, o_sem.at[0]).wait()
    arrived(next_hbm, b0_recv.at[2])
    arrived(nrouter_hbm, b0_recv.at[3])
    arrived(next_sums.at[0], next_sem.at[0])
    arrived(next_sums.at[1], next_sem.at[1])
    total = next_sums[0] + next_sums[1]
    token = [
        jnp.dot(total[e, :, 0 : groups * ROWS], next_sel[e], preferred_element_type=F32, precision=HIGHEST)[0:1]
        for e in range(EXPERTS)
    ]
    token = jnp.concatenate(token * 2, axis=0)
    gate = next_gate[...]
    mixed = jnp.sum((gate * token)[0:EXPERTS], axis=0, keepdims=True)
    spread_ref[...] = gate * (token - mixed)
    three = pl.ds(0, 3)
    na = len(A_CHUNKS)
    for kind, ref in enumerate(
        (
            packed.at[:, three], packed_z.at[:, three], rows.at[pl.ds(0, na), 0, :, three], raw_z.at[:, three],
            rows.at[:, 0], info.at[three], gs.at[three], gt.at[three], x2.at[pl.ds(0, 128), :], pts.at[pl.ds(0, 15)],
            info.at[0, 0], logits.at[0], next_hbm, nrouter_hbm, next_logits, next_ids, next_sums,
        )
    ):
        drain(ref, kind)


def expert_call(tokens, ids, logits, saved, weight, router):
    depth, hidden = tokens.shape[-1], weight.shape[0]
    groups = saved.shape[0]
    width = depth // 2 // NC
    dma = pltpu.SemaphoreType.DMA
    anywhere = pl.BlockSpec(memory_space=pl.ANY)
    na, nb = len(A_CHUNKS), len(B_CHUNKS)
    return pl.pallas_call(
        functools.partial(expert_kernel, groups, width),
        name="experts",
        out_shape=(
            jax.ShapeDtypeStruct((groups, 256, hidden), BF16),
            jax.ShapeDtypeStruct(tokens.shape, BF16),
            jax.ShapeDtypeStruct(router.shape, F32),
            jax.ShapeDtypeStruct((8, 128), F32),
        ),
        in_specs=[anywhere] * 6,
        out_specs=(anywhere, anywhere, anywhere, pl.BlockSpec(memory_space=pltpu.VMEM)),
        scratch_shapes=[
            pltpu.VMEM((NC, 2, groups, NZ, NX, ROWS, width), BF16),
            pltpu.VMEM((HELD, 2, hidden, width), BF16),
            pltpu.VMEM((groups, 256, hidden), F32),
            pltpu.VMEM((groups, 256, hidden), BF16),
            pltpu.VMEM((256, depth // 2), BF16),
            pltpu.VMEM((NZ, 2) + ids.shape, jnp.int32),
            pltpu.VMEM((2,) + ids.shape, F32),
            pltpu.VMEM((NZ, EXPERTS, groups * ROWS, 256), BF16),
            pltpu.VMEM((na, EXPERTS, groups, ROWS, width), BF16),
            pltpu.VMEM((nb, NZ, 256, width), BF16),
            pltpu.VMEM((nb, EXPERTS, groups, NZ, ROWS, width), BF16),
            pltpu.VMEM((EXPERTS, 8, 256), F32),
            pltpu.VMEM((NZ, NX, 8, 256), F32),
            pltpu.VMEM((8, 128), F32),
            pltpu.VMEM((EXPERTS, groups * ROWS, 128), F32),
            pltpu.VMEM(ids.shape, jnp.int32),
            pltpu.VMEM(ids.shape, F32),
            pltpu.VMEM((16, 8, 256), F32),
            pltpu.VMEM((16, 8, 256), F32),
            pltpu.VMEM((EXPERTS, 8, 256), F32),
            pltpu.VMEM((2, EXPERTS, 8, 256), F32),
            dma((PIECES + 2,)), dma((HELD,)), dma((1,)), dma((1,)), dma((NC + 2,)), dma((17,)), dma((6 + PIECES,)),
            dma((na + 1, 3)), dma((nb, 3, 3)), dma((NC + 2, 3)), dma((NC, 3)), dma((15,)), dma((2,)),
        ],
        compiler_params=pltpu.CompilerParams(
            collective_id=0, has_side_effects=True, vmem_limit_bytes=67043328
        ),
        cost_estimate=pl.CostEstimate(
            flops=2 * groups * 256 * depth * hidden, bytes_accessed=200_000_000, transcendentals=0
        ),
    )(tokens, ids, logits, saved, weight, router)


def last_kernel(
    grad_hbm, tokens_hbm, router_ref, spread_ref, hidden_hbm, upstream_hbm,
    grad, tokens, upstream, grad_in, grad_out, token_in, token_out,
):
    groups, pieces = grad.shape[0], tokens.shape[0]
    width = tokens.shape[2]
    reads, token_reads, writes = [], [], []
    for q in range(pieces):
        cols = pl.ds(q * width, width)
        token_reads.append(pltpu.make_async_copy(tokens_hbm.at[:, cols], tokens.at[q], token_in.at[q]))
        token_reads[q].start()
    for g in range(groups):
        reads.append(pltpu.make_async_copy(grad_hbm.at[g], grad.at[g], grad_in.at[g]))
        reads[g].start()

    def write(src, dst, sem):
        writes.append(pltpu.make_async_copy(src, dst, sem))
        writes[-1].start()

    live = lax.axis_index("section") < lax.axis_size("section") - 1
    spread = jnp.transpose(spread_ref[...])
    for q in range(pieces):
        token_reads[q].wait()
        total = tokens[q].astype(F32)
        for e in range(EXPERTS):
            total = total + spread[:, e : e + 1] * router_ref[e : e + 1, q * width : (q + 1) * width]
        upstream[q] = jnp.where(live, total, 0.0).astype(BF16)
        write(upstream.at[q], upstream_hbm.at[:, pl.ds(q * width, width)], token_out.at[q])
        for g in range(q * groups // pieces, (q + 1) * groups // pieces):
            reads[g].wait()
            write(grad.at[g], hidden_hbm.at[g], grad_out.at[g])
    for copy in writes:
        copy.wait()


def last_call(grad, tokens, router, spread):
    groups = grad.shape[0]
    flat, depth = tokens.shape
    pieces = 4
    anywhere = pl.BlockSpec(memory_space=pl.ANY)
    whole = pl.BlockSpec(memory_space=pltpu.VMEM)
    dma = pltpu.SemaphoreType.DMA
    return pl.pallas_call(
        last_kernel,
        name="last",
        out_shape=(jax.ShapeDtypeStruct(grad.shape, BF16), jax.ShapeDtypeStruct(tokens.shape, BF16)),
        in_specs=[anywhere, anywhere, whole, whole],
        out_specs=(anywhere, anywhere),
        scratch_shapes=[
            pltpu.VMEM(grad.shape, BF16),
            pltpu.VMEM((pieces, flat, depth // pieces), BF16),
            pltpu.VMEM((pieces, flat, depth // pieces), BF16),
            dma((groups,)), dma((groups,)), dma((pieces,)), dma((pieces,)),
        ],
        compiler_params=pltpu.CompilerParams(vmem_limit_bytes=67043328),
    )(grad, tokens, router, spread)


def local(upstream_dy, gate_logits, expert_ids, saved_hidden, down_weight, router_weight):
    micro, per, depth = upstream_dy.shape[1:]
    hidden = down_weight.shape[1]
    flat = micro * per
    saved = saved_hidden[0].transpose(0, 2, 1, 3).reshape(micro * CAP // 8, 256, hidden)
    grad, tokens, router, spread = expert_call(
        upstream_dy[0].reshape(flat, depth), expert_ids[0].transpose(0, 2, 1), gate_logits[0].transpose(0, 2, 1), saved, down_weight[0], router_weight[0].T
    )
    hidden_grad, upstream = last_call(grad, tokens, router, spread)
    hidden_grad = hidden_grad.reshape(micro, CAP, NX * NZ * 2, hidden).transpose(0, 2, 1, 3)
    return (hidden_grad[None], upstream.reshape(micro, per, depth)[None])


def solution(mesh):
    placed = (
        P("section", None, "expert", None),
        P("section", None, "expert", None),
        P("section", None, "expert", None),
        P("section", None, None, None, "expert"),
        P("section", "expert", None),
        P("section", None, None),
    )
    return jax.shard_map(
        local,
        mesh=mesh,
        in_specs=placed,
        out_specs=(P("section", None, None, None, "expert"), P("section", None, "expert", None)),
        check_vma=False,
    )
```

```python
import functools

import jax
import jax.numpy as jnp
from jax import lax
from jax.experimental import pallas as pl
from jax.experimental.pallas import tpu as pltpu
from jax.sharding import PartitionSpec as P

EXPERTS = 4
CAP = 36
NX = 4
NZ = 4
NC = 12
A_CHUNKS = (0, 2, 4, 6, 8, 10, 11)
B_CHUNKS = (1, 3, 5, 7, 9)
PASSES = ((1, 0), (3, 2), (4, 5), (6,), (7,), (8,), (10,))
ORDER = (1, 0, 3, 2, 4, 5, 6, 7, 8, 10, 9, 11)
THIRDS = 9
HELD = 6
PIECES = 4
FIRST = (
    "u1", "g12", "x12", "t1", "p0", "p2", "x0", "t3", "t5", "p4", "x2", "t7",
    "p6", "x4", "p8", "x6", "t9", "p10", "x8", "p11", "x10", "x11",
)
EARLY = (
    "r1", "r3", "a0", "r5", "c1", "r7", "c3", "r9", "a2", "c5", "c7", "c9",
)
LATE = (
    "n0", "s0", "a4", "w101", "w201", "n2", "a6", "w301", "s2", "f0", "m0", "n4",
    "a8", "w103", "w203", "s4", "w303", "f2", "m1", "n6", "a10", "w105", "w205", "f4",
    "s6", "w305", "n8", "m2", "w107", "f6", "s8", "w207", "m3", "n10", "a11", "w307",
    "s10", "m4", "f8", "f10", "w109", "m5", "w209", "m109", "n11", "s11", "m6", "w309",
    "m209", "f11", "m309",
)
ROWS = 16
MESH = pl.DeviceIdType.MESH
F32 = jnp.float32
BF16 = jnp.bfloat16
NT = (((1,), (1,)), ((), ()))
HIGHEST = lax.Precision.HIGHEST


def permutation(turned):
    i = lax.broadcasted_iota(jnp.int32, (256, 256), 1 if turned else 0)
    n = lax.broadcasted_iota(jnp.int32, (256, 256), 0 if turned else 1)
    z, x, src, slot = i >> 6, (i >> 4) & 3, (i >> 3) & 1, i & 7
    return (n == slot * 32 + (x * 4 + z) * 2 + src).astype(F32).astype(BF16)


def codes_of(ids, logits, src):
    chosen = [jnp.concatenate([ids[0, k : k + 1], ids[1, k : k + 1]], axis=1) for k in range(2)]
    picks = [[(row == e).astype(F32) for e in range(EXPERTS)] for row in chosen]
    picked = jnp.concatenate([a + b for a, b in zip(*picks)] * 2, axis=0)
    t = lax.broadcasted_iota(jnp.int32, (128, 128), 0)
    u = lax.broadcasted_iota(jnp.int32, (128, 128), 1)
    earlier = ((t < u) & ((t >> 6) == (u >> 6))).astype(F32).astype(BF16)
    rank = jnp.dot(picked.astype(BF16), earlier, preferred_element_type=F32)
    micro = (lax.broadcasted_iota(jnp.int32, (8, 128), 1) >> 6).astype(F32)
    slot = rank + micro * CAP
    base = jnp.floor(slot * 0.125)
    code = jnp.where(picked > 0, base * 8 + slot + src * 8, -1.0)
    if logits is None:
        return code, None
    logit = [jnp.concatenate([logits[0, k : k + 1], logits[1, k : k + 1]], axis=1) for k in range(2)]
    diff = logit[0] - logit[1]
    first, second = jax.nn.sigmoid(diff), jax.nn.sigmoid(-diff)
    gate = jnp.concatenate([a * first + b * second for a, b in zip(*picks)] * 2, axis=0)
    return code, gate


def expert_kernel(
    groups, width, x_hbm, ids_hbm, logits_hbm, saved_hbm, w_hbm, router_hbm, grad_hbm, next_hbm, nrouter_hbm, spread_ref,
    rows, wv, acc, sv, x2, info, logits, selz, packed, raw_z, packed_z, gs, gt, next_gate, next_sel, next_ids, next_logits, pts, pr, sums, next_sums,
    x_sem, w_sem, s_sem, o_sem, loc_sem, sent, b0_recv, xa, xb, zr, br, pr_sem, next_sem,
):
    me = lax.axis_index("expert")
    section = lax.axis_index("section")
    mx, mz, mc = me // 8, (me // 2) % 4, me % 2
    half = width * NC

    def dev(x, z, c, s=0):
        index = (lax.rem(x + 8, NX) * NZ + lax.rem(z + 8, NZ)) * 2 + c
        return (lax.rem(section + s + 4, 4), index)

    sibling = dev(mx, mz, 1 - mc)
    xdev = [dev(mx + d, mz, mc) for d in range(NX)]
    zdev = [dev(mx, mz + d, mc) for d in range(NZ)]
    before, after = dev(mx, mz, mc, -1), dev(mx, mz, mc, 1)
    before_other, after_other = dev(mx, mz, 1 - mc, -1), dev(mx, mz, 1 - mc, 1)
    chips = [(dx, dz) for dx in range(NX) for dz in range(NZ) if dx or dz]

    def remote(src, dst, send, recv, target):
        return pltpu.make_async_remote_copy(
            src_ref=src, dst_ref=dst, send_sem=send, recv_sem=recv, device_id=target, device_id_type=MESH
        )

    def send(src, dst, recv_sem, target, kind):
        remote(src, dst, sent.at[kind], recv_sem, target).start()

    def drain(ref, kind):
        remote(ref, ref, sent.at[kind], b0_recv.at[0], sibling).wait_send()

    def arrived(ref, sem):
        remote(ref, ref, sent.at[0], sem, sibling).wait_recv()

    mine_rows = pl.ds(pl.multiple_of(mc * 128, 128), 128)
    sib_rows = pl.ds(pl.multiple_of((1 - mc) * 128, 128), 128)
    own_c = pltpu.make_async_copy(ids_hbm, info.at[mz, mc], x_sem.at[PIECES])
    own_c.start()
    own_l = pltpu.make_async_copy(logits_hbm, logits.at[mc], x_sem.at[PIECES + 1])
    own_l.start()
    piece = half // PIECES
    own_x = []
    for q in range(PIECES):
        cols = pl.ds(pl.multiple_of(mc * half + q * piece, 128), piece)
        own_x.append(
            pltpu.make_async_copy(x_hbm.at[:, cols], x2.at[mine_rows, q * piece : (q + 1) * piece], x_sem.at[q])
        )
        own_x[q].start()

    barrier = pltpu.get_barrier_semaphore()
    partners = [sibling, before, after, before_other, after_other] + [dev(mx + dx, mz + dz, mc) for dx, dz in chips]
    for target in partners:
        pl.semaphore_signal(barrier, inc=1, device_id=target, device_id_type=MESH)
    pl.semaphore_wait(barrier, len(partners))

    send(ids_hbm, info.at[mz, mc], b0_recv.at[1], sibling, 10)
    send(logits_hbm, logits.at[mc], b0_recv.at[0], sibling, 11)
    for q in range(PIECES):
        cols = pl.ds(pl.multiple_of((1 - mc) * half + q * piece, 128), piece)
        to = x2.at[mine_rows, q * piece : (q + 1) * piece]
        send(x_hbm.at[:, cols], to, b0_recv.at[6 + q], sibling, 8)
    swapped = set()

    def swap_done(k):
        q = k * width // piece
        if q not in swapped:
            swapped.add(q)
            own_x[q].wait()
            arrived(x2.at[sib_rows, q * piece : (q + 1) * piece], b0_recv.at[6 + q])

    def w_copies(k):
        slot = ORDER.index(k) % HELD
        copies = []
        for h in range(2):
            cols = pl.ds(h * half + k * width, width)
            copies.append(pltpu.make_async_copy(w_hbm.at[:, cols], wv.at[slot, h], w_sem.at[slot]))
        return copies

    for k in ORDER[:HELD]:
        for copy in w_copies(k):
            copy.start()
    s_copy = [pltpu.make_async_copy(saved_hbm, sv, s_sem.at[0])]
    s_copy[0].start()
    send(ids_hbm, next_ids, b0_recv.at[4], before, 15)
    send(logits_hbm, next_logits, b0_recv.at[5], before, 14)
    send(x_hbm, next_hbm, b0_recv.at[2], before, 12)
    send(router_hbm, nrouter_hbm, b0_recv.at[3], before, 13)

    def select(z, own=False):
        code0, gate0 = codes_of(info[z, 0], logits[0] if own else None, 0)
        code1, gate1 = codes_of(info[z, 1], logits[1] if own else None, 1)
        row = lax.broadcasted_iota(jnp.int32, (groups * ROWS, 256), 0).astype(F32)
        gates = []
        for e in range(EXPERTS):
            code = jnp.concatenate([code0[e : e + 1], code1[e : e + 1]], axis=1)
            selz[z, e] = (row == code).astype(F32).astype(BF16)
            if own:
                gates.append(jnp.concatenate([gate0[e : e + 1], gate1[e : e + 1]], axis=1))
        return gates

    gs[...] = jnp.zeros_like(gs)

    def own_select(_):
        own_c.wait()
        own_l.wait()
        arrived(info.at[mz, 1 - mc], b0_recv.at[1])
        arrived(logits.at[1 - mc], b0_recv.at[0])
        for d in (1, 3, 2):
            send(info.at[mz], info.at[mz], zr.at[NC + 1, d - 1], zdev[d], 5)
        gates = select(mz, True)
        for e in range(EXPERTS):
            gs[e, :, 0 : groups * ROWS] = lax.dot_general(
                jnp.broadcast_to(gates[e], (8, 256)).astype(BF16), selz[mz, e], NT, preferred_element_type=F32
            )

    def columns(k):
        return slice(k * width, (k + 1) * width)

    third = groups // 3

    parts = [pl.ds(p * third, third) for p in range(3)]

    def start_raw(k):
        b = B_CHUNKS.index(k)
        swap_done(k)
        for d in (1, 3):
            if k == B_CHUNKS[0]:
                send(x2.at[sib_rows, columns(k)], raw_z.at[b, mz, sib_rows], zr.at[k, d - 1], zdev[d], 3)
            else:
                send(x2.at[:, columns(k)], raw_z.at[b, mz], zr.at[k, d - 1], zdev[d], 3)

    def start_own(k):
        b = B_CHUNKS.index(k)
        cols = pl.ds(pl.multiple_of(mc * half + k * width, 128), width)
        for d in (1, 3):
            send(x_hbm.at[:, cols], raw_z.at[b, mz, mine_rows], zr.at[k, d - 1], zdev[d], 3)

    def relay_raw(k):
        b = B_CHUNKS.index(k)
        for d, part in ((1, pl.ds(0, 128)), (3, pl.ds(128, 128))):
            z = lax.rem(mz - d + NZ, NZ)
            arrived(raw_z.at[b, z], zr.at[k, d - 1])
            ref = raw_z.at[b, z, part]
            send(ref, ref, zr.at[k, 1], zdev[d], 3)

    def pack(k):
        a = A_CHUNKS.index(k)
        swap_done(k)
        for e in range(EXPERTS):
            block = jnp.dot(selz[mz, e], x2[:, columns(k)], preferred_element_type=F32)
            packed[a, e] = block.astype(BF16).reshape(groups, ROWS, width)

    locals_ = {}

    def start_x(k):
        if k == NC:
            locals_[k] = pltpu.make_async_copy(gs.at[mx], gt.at[mz, mx], loc_sem.at[k])
        elif k in A_CHUNKS:
            locals_[k] = pltpu.make_async_copy(
                packed.at[A_CHUNKS.index(k), mx], rows.at[k, mc, :, mz, mx], loc_sem.at[k]
            )
        else:
            locals_[k] = pltpu.make_async_copy(
                packed_z.at[B_CHUNKS.index(k), mx], rows.at[k, mc, :, :, mx], loc_sem.at[k]
            )
        locals_[k].start()
        for p, at in enumerate(parts if k in B_CHUNKS else parts[:1]):
            for d in (2, 1, 3):
                e = lax.rem(mx + d, NX)
                if k == NC:
                    send(gs.at[e], gt.at[mz, mx], xa.at[len(A_CHUNKS), d - 1], xdev[d], 6)
                elif k in A_CHUNKS:
                    a = A_CHUNKS.index(k)
                    send(packed.at[a, e], rows.at[k, mc, :, mz, mx], xa.at[a, d - 1], xdev[d], 0)
                else:
                    b = B_CHUNKS.index(k)
                    send(packed_z.at[b, e, at], rows.at[k, mc, at, :, mx], xb.at[b, d - 1, p], xdev[d], 1)

    def around_z(k):
        locals_[k].wait()
        for d in (1, 2, 3):
            x = lax.rem(mx - d + NX, NX)
            a = len(A_CHUNKS) if k == NC else A_CHUNKS.index(k)
            arrived(gt.at[mz, x] if k == NC else rows.at[k, mc, :, mz, x], xa.at[a, d - 1])
        if k == NC:
            for d in (1, 3, 2):
                send(gt.at[mz], gt.at[mz], zr.at[k, d - 1], zdev[d], 7)
            return
        ref = rows.at[k, mc, :, mz]
        for d in (1, 3):
            send(ref, ref, zr.at[k, d - 1], zdev[d], 2)
        send(ref, ref, br.at[k, 0], sibling, 4)

    def cross_x(k):
        b = B_CHUNKS.index(k)
        opposite = lax.rem(mz + 2, NZ)
        arrived(raw_z.at[b, opposite], zr.at[k, 1])
        for d in range(NZ):
            z = lax.rem(mz + d, NZ)
            tokens = raw_z[b, z] if d else x2[:, columns(k)]
            for e in range(EXPERTS):
                block = jnp.dot(selz[z, e], tokens, preferred_element_type=F32)
                packed_z[b, e, :, z] = block.astype(BF16).reshape(groups, ROWS, width)
        start_x(k)

    def near(k):
        for d, share in ((1, pl.ds(0, 2)), (3, pl.ds(2, 2))):
            z = lax.rem(mz - d + NZ, NZ)
            arrived(rows.at[k, mc, :, z], zr.at[k, d - 1])
            ref = rows.at[k, mc, :, z, share]
            send(ref, ref, zr.at[k, 1], zdev[d], 2)

    def near_shared(k):
        for d in (1, 3):
            ref = rows.at[k, mc, :, lax.rem(mz - d + NZ, NZ)]
            send(ref, ref, br.at[k, 0], sibling, 4)

    def far(k):
        ref = rows.at[k, mc, :, lax.rem(mz + 2, NZ)]
        arrived(ref, zr.at[k, 1])
        send(ref, ref, br.at[k, 0], sibling, 4)

    def whole(step):
        k, p = step % 100, step // 100 - 1
        b, at = B_CHUNKS.index(k), parts[p]
        if p == 0:
            locals_[k].wait()
        for d in (1, 2, 3):
            arrived(rows.at[k, mc, at, :, lax.rem(mx - d + NX, NX)], xb.at[b, d - 1, p])
        send(rows.at[k, mc, at], rows.at[k, mc, at], br.at[k, p if k == THIRDS else 0], sibling, 4)

    def shared(k):
        arrived(rows.at[k, 1 - mc], br.at[k, 0])

    def terms(ks, at):
        total = None
        for k in ks:
            slot = ORDER.index(k) % HELD
            for h in range(2):
                left = rows[k, h, at].reshape(third * 256, width)
                term = lax.dot_general(left, wv[slot, h], NT, preferred_element_type=F32)
                total = term if total is None else total + term
        return total.reshape(third, 256, total.shape[-1])

    def w_ready(k):
        slot = ORDER.index(k) % HELD
        pltpu.make_async_copy(wv.at[slot], wv.at[slot], w_sem.at[slot]).wait()

    def compute(step):
        if step >= 100:
            k, p = step % 100, step // 100 - 1
            arrived(rows.at[k, 1 - mc, parts[p]], br.at[k, p])
            if p == 0:
                w_ready(k)
            acc[parts[p]] += terms((k,), parts[p])
            return
        ks = PASSES[step]
        for k in ks:
            shared(k)
            w_ready(k)

        def body(m, carry):
            at = pl.ds(m * third, third)
            total = terms(ks, at)
            acc[at] = total if step == 0 else acc[at] + total
            return carry

        lax.fori_loop(0, 3, body, 0)
        for k in ks:
            later = ORDER.index(k) + HELD
            if later < len(ORDER):
                for copy in w_copies(ORDER[later]):
                    copy.start()

    def in_order(names):
        steps = {
            "u": start_own, "t": start_raw, "r": relay_raw, "c": cross_x, "g": own_select, "p": pack, "x": start_x, "a": around_z,
            "n": near, "f": far, "w": whole, "m": compute, "s": near_shared,
        }
        for word in names:
            steps[word[0]](int(word[1:]))

    in_order(FIRST)
    around_z(NC)
    for d in (1, 2, 3):
        z = lax.rem(mz + d, NZ)
        arrived(info.at[z], zr.at[NC + 1, NZ - d - 1])
        select(z)
    in_order(EARLY)
    perm = permutation(False)

    def place_saved(g, carry):
        sv[g] = jnp.dot(perm, sv[g], preferred_element_type=F32).astype(BF16)
        return carry

    arrived(next_ids, b0_recv.at[4])
    arrived(next_logits, b0_recv.at[5])
    code, gate = codes_of(next_ids, next_logits, mc.astype(F32))
    next_gate[...] = gate
    row = lax.broadcasted_iota(jnp.int32, (groups * ROWS, 128), 0).astype(F32)
    for e in range(EXPERTS):
        next_sel[e] = (row == code[e : e + 1]).astype(F32)
    for copy in s_copy:
        copy.wait()
    lax.fori_loop(0, groups, place_saved, 0)
    for d in (1, 2, 3):
        arrived(gt.at[lax.rem(mz - d + NZ, NZ)], zr.at[NC, d - 1])
    in_order(LATE)
    lane = lax.broadcasted_iota(jnp.int32, (256, 256), 1)
    row16 = lax.broadcasted_iota(jnp.int32, (256, 256), 0) & 15

    shared(ORDER[-1])
    w_ready(ORDER[-1])

    def dots(m, total):
        at = pl.ds(m * third, third)
        raw = acc[at] + terms(ORDER[-1:], at)
        acc[at] = raw
        part = jnp.sum(raw * sv[at].astype(F32), axis=2, keepdims=True)
        for n in range(third):
            placed = jnp.where(lane == row16 + (m * third + n) * 16, part[n], 0.0)
            total = total + jnp.sum(placed.reshape(16, 16, 256), axis=1)
        return total

    part = lax.fori_loop(0, 3, dots, jnp.zeros((16, 256), F32))
    pts[...] = jnp.broadcast_to(part[:, None, :], (16, 8, 256))
    slot = mx * NZ + mz
    own_part = pltpu.make_async_copy(pts.at[mz * NX + mx], pr.at[slot], loc_sem.at[NC + 1])
    own_part.start()
    for n, (dx, dz) in enumerate(chips):
        x, z = lax.rem(mx + dx, NX), lax.rem(mz + dz, NZ)
        send(pts.at[z * NX + x], pr.at[slot], pr_sem.at[n], dev(x, z, mc), 9)

    gates = jnp.broadcast_to(gt[...].reshape(16, 8, 256)[:, 0:1, :], (16, 16, 256)).reshape(256, 256)

    back = permutation(True)

    def finish(g, carry):
        gate = jnp.sum(jnp.where(lane == row16 + g * 16, gates, 0.0), axis=1, keepdims=True)
        grad = (gate * acc[g]).astype(BF16)
        sv[g] = jnp.dot(back, grad, preferred_element_type=F32).astype(BF16)
        pltpu.make_async_copy(sv.at[g], grad_hbm.at[g], o_sem.at[0]).start()
        return carry

    lax.fori_loop(0, groups, finish, 0)

    own_part.wait()
    for n, (dx, dz) in enumerate(chips):
        x, z = lax.rem(mx - dx + NX, NX), lax.rem(mz - dz + NZ, NZ)
        arrived(pr.at[x * NZ + z], pr_sem.at[n])
    summed = jnp.sum(pr[...].reshape(EXPERTS, NZ, 8, 256), axis=1)
    sums[...] = summed
    send(sums, next_sums.at[mc], next_sem.at[mc], before, 16)
    send(sums, next_sums.at[mc], next_sem.at[mc], before_other, 16)
    pltpu.make_async_copy(sv, grad_hbm, o_sem.at[0]).wait()
    arrived(next_hbm, b0_recv.at[2])
    arrived(nrouter_hbm, b0_recv.at[3])
    arrived(next_sums.at[0], next_sem.at[0])
    arrived(next_sums.at[1], next_sem.at[1])
    total = next_sums[0] + next_sums[1]
    token = [
        jnp.dot(total[e, :, 0 : groups * ROWS], next_sel[e], preferred_element_type=F32, precision=HIGHEST)[0:1]
        for e in range(EXPERTS)
    ]
    token = jnp.concatenate(token * 2, axis=0)
    gate = next_gate[...]
    mixed = jnp.sum((gate * token)[0:EXPERTS], axis=0, keepdims=True)
    spread_ref[...] = gate * (token - mixed)
    three = pl.ds(0, 3)
    na = len(A_CHUNKS)
    for kind, ref in enumerate(
        (
            packed.at[:, three], packed_z.at[:, three], rows.at[pl.ds(0, na), 0, :, three], raw_z.at[:, three],
            rows.at[:, 0], info.at[three], gs.at[three], gt.at[three], x2.at[pl.ds(0, 128), :], pts.at[pl.ds(0, 15)],
            info.at[0, 0], logits.at[0], next_hbm, nrouter_hbm, next_logits, next_ids, next_sums,
        )
    ):
        drain(ref, kind)


def expert_call(tokens, ids, logits, saved, weight, router):
    depth, hidden = tokens.shape[-1], weight.shape[0]
    groups = saved.shape[0]
    width = depth // 2 // NC
    dma = pltpu.SemaphoreType.DMA
    anywhere = pl.BlockSpec(memory_space=pl.ANY)
    na, nb = len(A_CHUNKS), len(B_CHUNKS)
    return pl.pallas_call(
        functools.partial(expert_kernel, groups, width),
        name="experts",
        out_shape=(
            jax.ShapeDtypeStruct((groups, 256, hidden), BF16),
            jax.ShapeDtypeStruct(tokens.shape, BF16),
            jax.ShapeDtypeStruct(router.shape, F32),
            jax.ShapeDtypeStruct((8, 128), F32),
        ),
        in_specs=[anywhere] * 6,
        out_specs=(anywhere, anywhere, anywhere, pl.BlockSpec(memory_space=pltpu.VMEM)),
        scratch_shapes=[
            pltpu.VMEM((NC, 2, groups, NZ, NX, ROWS, width), BF16),
            pltpu.VMEM((HELD, 2, hidden, width), BF16),
            pltpu.VMEM((groups, 256, hidden), F32),
            pltpu.VMEM((groups, 256, hidden), BF16),
            pltpu.VMEM((256, depth // 2), BF16),
            pltpu.VMEM((NZ, 2) + ids.shape, jnp.int32),
            pltpu.VMEM((2,) + ids.shape, F32),
            pltpu.VMEM((NZ, EXPERTS, groups * ROWS, 256), BF16),
            pltpu.VMEM((na, EXPERTS, groups, ROWS, width), BF16),
            pltpu.VMEM((nb, NZ, 256, width), BF16),
            pltpu.VMEM((nb, EXPERTS, groups, NZ, ROWS, width), BF16),
            pltpu.VMEM((EXPERTS, 8, 256), F32),
            pltpu.VMEM((NZ, NX, 8, 256), F32),
            pltpu.VMEM((8, 128), F32),
            pltpu.VMEM((EXPERTS, groups * ROWS, 128), F32),
            pltpu.VMEM(ids.shape, jnp.int32),
            pltpu.VMEM(ids.shape, F32),
            pltpu.VMEM((16, 8, 256), F32),
            pltpu.VMEM((16, 8, 256), F32),
            pltpu.VMEM((EXPERTS, 8, 256), F32),
            pltpu.VMEM((2, EXPERTS, 8, 256), F32),
            dma((PIECES + 2,)), dma((HELD,)), dma((1,)), dma((1,)), dma((NC + 2,)), dma((17,)), dma((6 + PIECES,)),
            dma((na + 1, 3)), dma((nb, 3, 3)), dma((NC + 2, 3)), dma((NC, 3)), dma((15,)), dma((2,)),
        ],
        compiler_params=pltpu.CompilerParams(
            collective_id=0, has_side_effects=True, vmem_limit_bytes=67043328
        ),
        cost_estimate=pl.CostEstimate(
            flops=2 * groups * 256 * depth * hidden, bytes_accessed=200_000_000, transcendentals=0
        ),
    )(tokens, ids, logits, saved, weight, router)


def last_kernel(
    grad_hbm, tokens_hbm, router_ref, spread_ref, hidden_hbm, upstream_hbm,
    grad, tokens, upstream, grad_in, grad_out, token_in, token_out,
):
    groups, pieces = grad.shape[0], tokens.shape[0]
    width = tokens.shape[2]
    reads, token_reads, writes = [], [], []
    for q in range(pieces):
        cols = pl.ds(q * width, width)
        token_reads.append(pltpu.make_async_copy(tokens_hbm.at[:, cols], tokens.at[q], token_in.at[q]))
        token_reads[q].start()
    for g in range(groups):
        reads.append(pltpu.make_async_copy(grad_hbm.at[g], grad.at[g], grad_in.at[g]))
        reads[g].start()

    def write(src, dst, sem):
        writes.append(pltpu.make_async_copy(src, dst, sem))
        writes[-1].start()

    live = lax.axis_index("section") < lax.axis_size("section") - 1
    spread = jnp.transpose(spread_ref[...])
    for q in range(pieces):
        token_reads[q].wait()
        total = tokens[q].astype(F32)
        for e in range(EXPERTS):
            total = total + spread[:, e : e + 1] * router_ref[e : e + 1, q * width : (q + 1) * width]
        upstream[q] = jnp.where(live, total, 0.0).astype(BF16)
        write(upstream.at[q], upstream_hbm.at[:, pl.ds(q * width, width)], token_out.at[q])
        for g in range(q * groups // pieces, (q + 1) * groups // pieces):
            reads[g].wait()
            write(grad.at[g], hidden_hbm.at[g], grad_out.at[g])
    for copy in writes:
        copy.wait()


def last_call(grad, tokens, router, spread):
    groups = grad.shape[0]
    flat, depth = tokens.shape
    pieces = 4
    anywhere = pl.BlockSpec(memory_space=pl.ANY)
    whole = pl.BlockSpec(memory_space=pltpu.VMEM)
    dma = pltpu.SemaphoreType.DMA
    return pl.pallas_call(
        last_kernel,
        name="last",
        out_shape=(jax.ShapeDtypeStruct(grad.shape, BF16), jax.ShapeDtypeStruct(tokens.shape, BF16)),
        in_specs=[anywhere, anywhere, whole, whole],
        out_specs=(anywhere, anywhere),
        scratch_shapes=[
            pltpu.VMEM(grad.shape, BF16),
            pltpu.VMEM((pieces, flat, depth // pieces), BF16),
            pltpu.VMEM((pieces, flat, depth // pieces), BF16),
            dma((groups,)), dma((groups,)), dma((pieces,)), dma((pieces,)),
        ],
        compiler_params=pltpu.CompilerParams(vmem_limit_bytes=67043328),
    )(grad, tokens, router, spread)


def local(upstream_dy, gate_logits, expert_ids, saved_hidden, down_weight, router_weight):
    micro, per, depth = upstream_dy.shape[1:]
    hidden = down_weight.shape[1]
    flat = micro * per
    saved = saved_hidden[0].transpose(0, 2, 1, 3).reshape(micro * CAP // 8, 256, hidden)
    grad, tokens, router, spread = expert_call(
        upstream_dy[0].reshape(flat, depth), expert_ids[0].transpose(0, 2, 1), gate_logits[0].transpose(0, 2, 1), saved, down_weight[0], router_weight[0].T
    )
    hidden_grad, upstream = last_call(grad, tokens, router, spread)
    hidden_grad = hidden_grad.reshape(micro, CAP, NX * NZ * 2, hidden).transpose(0, 2, 1, 3)
    return (hidden_grad[None], upstream.reshape(micro, per, depth)[None])


def solution(mesh):
    placed = (
        P("section", None, "expert", None),
        P("section", None, "expert", None),
        P("section", None, "expert", None),
        P("section", None, None, None, "expert"),
        P("section", "expert", None),
        P("section", None, None),
    )
    return jax.shard_map(
        local,
        mesh=mesh,
        in_specs=placed,
        out_specs=(P("section", None, None, None, "expert"), P("section", None, "expert", None)),
        check_vma=False,
    )
```

```python
import functools

import jax
import jax.numpy as jnp
from jax import lax
from jax.experimental import pallas as pl
from jax.experimental.pallas import tpu as pltpu
from jax.sharding import PartitionSpec as P

EXPERTS = 4
CAP = 36
NX = 4
NZ = 4
NC = 12
A_CHUNKS = (0, 2, 4, 6, 8, 10, 11)
B_CHUNKS = (1, 3, 5, 7, 9)
PASSES = ((1, 0), (3, 2), (4, 5), (6,), (7,), (8,), (10,))
ORDER = (1, 0, 3, 2, 4, 5, 6, 7, 8, 10, 9, 11)
THIRDS = 9
HELD = 6
PIECES = 4
FIRST = (
    "u1", "g12", "x12", "t1", "p0", "p2", "x0", "t3", "t5", "p4", "x2", "t7",
    "p6", "x4", "p8", "x6", "t9", "p10", "x8", "p11", "x10", "x11",
)
EARLY = (
    "r1", "r3", "a0", "r5", "c1", "r7", "c3", "r9", "a2", "c5", "c7", "c9",
)
LATE = (
    "n0", "s0", "a4", "w101", "w201", "n2", "a6", "w301", "s2", "f0", "m0", "n4",
    "a8", "w103", "w203", "s4", "w303", "f2", "m1", "n6", "a10", "w105", "w205", "f4",
    "s6", "w305", "n8", "m2", "w107", "f6", "s8", "w207", "m3", "n10", "a11", "w307",
    "s10", "m4", "f8", "f10", "w109", "m5", "w209", "m109", "n11", "s11", "m6", "w309",
    "m209", "f11", "m309",
)
ROWS = 16
MESH = pl.DeviceIdType.MESH
F32 = jnp.float32
BF16 = jnp.bfloat16
NT = (((1,), (1,)), ((), ()))
HIGHEST = lax.Precision.HIGHEST


def permutation(turned):
    i = lax.broadcasted_iota(jnp.int32, (256, 256), 1 if turned else 0)
    n = lax.broadcasted_iota(jnp.int32, (256, 256), 0 if turned else 1)
    z, x, src, slot = i >> 6, (i >> 4) & 3, (i >> 3) & 1, i & 7
    return (n == slot * 32 + (x * 4 + z) * 2 + src).astype(F32).astype(BF16)


def codes_of(ids, logits, src):
    chosen = [jnp.concatenate([ids[0, k : k + 1], ids[1, k : k + 1]], axis=1) for k in range(2)]
    picks = [[(row == e).astype(F32) for e in range(EXPERTS)] for row in chosen]
    picked = jnp.concatenate([a + b for a, b in zip(*picks)] * 2, axis=0)
    t = lax.broadcasted_iota(jnp.int32, (128, 128), 0)
    u = lax.broadcasted_iota(jnp.int32, (128, 128), 1)
    earlier = ((t < u) & ((t >> 6) == (u >> 6))).astype(F32).astype(BF16)
    rank = jnp.dot(picked.astype(BF16), earlier, preferred_element_type=F32)
    micro = (lax.broadcasted_iota(jnp.int32, (8, 128), 1) >> 6).astype(F32)
    slot = rank + micro * CAP
    base = jnp.floor(slot * 0.125)
    code = jnp.where(picked > 0, base * 8 + slot + src * 8, -1.0)
    if logits is None:
        return code, None
    logit = [jnp.concatenate([logits[0, k : k + 1], logits[1, k : k + 1]], axis=1) for k in range(2)]
    diff = logit[0] - logit[1]
    first, second = jax.nn.sigmoid(diff), jax.nn.sigmoid(-diff)
    gate = jnp.concatenate([a * first + b * second for a, b in zip(*picks)] * 2, axis=0)
    return code, gate


def expert_kernel(
    groups, width, x_hbm, ids_hbm, logits_hbm, saved_hbm, w_hbm, router_hbm, grad_hbm, next_hbm, nrouter_hbm, spread_ref,
    rows, wv, acc, sv, x2, info, logits, selz, packed, raw_z, packed_z, gs, gt, next_gate, next_sel, next_ids, next_logits, pts, pr, sums, next_sums,
    x_sem, w_sem, s_sem, o_sem, loc_sem, sent, b0_recv, xa, xb, zr, br, pr_sem, next_sem,
):
    me = lax.axis_index("expert")
    section = lax.axis_index("section")
    mx, mz, mc = me // 8, (me // 2) % 4, me % 2
    half = width * NC

    def dev(x, z, c, s=0):
        index = (lax.rem(x + 8, NX) * NZ + lax.rem(z + 8, NZ)) * 2 + c
        return (lax.rem(section + s + 4, 4), index)

    sibling = dev(mx, mz, 1 - mc)
    xdev = [dev(mx + d, mz, mc) for d in range(NX)]
    zdev = [dev(mx, mz + d, mc) for d in range(NZ)]
    before, after = dev(mx, mz, mc, -1), dev(mx, mz, mc, 1)
    before_other, after_other = dev(mx, mz, 1 - mc, -1), dev(mx, mz, 1 - mc, 1)
    chips = [(dx, dz) for dx in range(NX) for dz in range(NZ) if dx or dz]

    def remote(src, dst, send, recv, target):
        return pltpu.make_async_remote_copy(
            src_ref=src, dst_ref=dst, send_sem=send, recv_sem=recv, device_id=target, device_id_type=MESH
        )

    def send(src, dst, recv_sem, target, kind):
        remote(src, dst, sent.at[kind], recv_sem, target).start()

    def drain(ref, kind):
        remote(ref, ref, sent.at[kind], b0_recv.at[0], sibling).wait_send()

    def arrived(ref, sem):
        remote(ref, ref, sent.at[0], sem, sibling).wait_recv()

    mine_rows = pl.ds(pl.multiple_of(mc * 128, 128), 128)
    sib_rows = pl.ds(pl.multiple_of((1 - mc) * 128, 128), 128)
    own_c = pltpu.make_async_copy(ids_hbm, info.at[mz, mc], x_sem.at[PIECES])
    own_c.start()
    own_l = pltpu.make_async_copy(logits_hbm, logits.at[mc], x_sem.at[PIECES + 1])
    own_l.start()
    piece = half // PIECES
    own_x = []
    for q in range(PIECES):
        cols = pl.ds(pl.multiple_of(mc * half + q * piece, 128), piece)
        own_x.append(
            pltpu.make_async_copy(x_hbm.at[:, cols], x2.at[mine_rows, q * piece : (q + 1) * piece], x_sem.at[q])
        )
        own_x[q].start()

    barrier = pltpu.get_barrier_semaphore()
    partners = [sibling, before, after, before_other, after_other] + xdev[1:] + zdev[1:]
    for target in partners:
        pl.semaphore_signal(barrier, inc=1, device_id=target, device_id_type=MESH)
    pl.semaphore_wait(barrier, len(partners))

    send(ids_hbm, info.at[mz, mc], b0_recv.at[1], sibling, 10)
    send(logits_hbm, logits.at[mc], b0_recv.at[0], sibling, 11)
    for q in range(PIECES):
        cols = pl.ds(pl.multiple_of((1 - mc) * half + q * piece, 128), piece)
        to = x2.at[mine_rows, q * piece : (q + 1) * piece]
        send(x_hbm.at[:, cols], to, b0_recv.at[6 + q], sibling, 8)
    swapped = set()

    def swap_done(k):
        q = k * width // piece
        if q not in swapped:
            swapped.add(q)
            own_x[q].wait()
            arrived(x2.at[sib_rows, q * piece : (q + 1) * piece], b0_recv.at[6 + q])

    def w_copies(k):
        slot = ORDER.index(k) % HELD
        copies = []
        for h in range(2):
            cols = pl.ds(h * half + k * width, width)
            copies.append(pltpu.make_async_copy(w_hbm.at[:, cols], wv.at[slot, h], w_sem.at[slot]))
        return copies

    for k in ORDER[:HELD]:
        for copy in w_copies(k):
            copy.start()
    s_copy = [pltpu.make_async_copy(saved_hbm, sv, s_sem.at[0])]
    s_copy[0].start()
    send(ids_hbm, next_ids, b0_recv.at[4], before, 15)
    send(logits_hbm, next_logits, b0_recv.at[5], before, 14)
    send(x_hbm, next_hbm, b0_recv.at[2], before, 12)
    send(router_hbm, nrouter_hbm, b0_recv.at[3], before, 13)

    def select(z, own=False):
        code0, gate0 = codes_of(info[z, 0], logits[0] if own else None, 0)
        code1, gate1 = codes_of(info[z, 1], logits[1] if own else None, 1)
        row = lax.broadcasted_iota(jnp.int32, (groups * ROWS, 256), 0).astype(F32)
        gates = []
        for e in range(EXPERTS):
            code = jnp.concatenate([code0[e : e + 1], code1[e : e + 1]], axis=1)
            selz[z, e] = (row == code).astype(F32).astype(BF16)
            if own:
                gates.append(jnp.concatenate([gate0[e : e + 1], gate1[e : e + 1]], axis=1))
        return gates

    gs[...] = jnp.zeros_like(gs)

    def own_select(_):
        own_c.wait()
        own_l.wait()
        arrived(info.at[mz, 1 - mc], b0_recv.at[1])
        arrived(logits.at[1 - mc], b0_recv.at[0])
        for d in (1, 3, 2):
            send(info.at[mz], info.at[mz], zr.at[NC + 1, d - 1], zdev[d], 5)
        gates = select(mz, True)
        for e in range(EXPERTS):
            gs[e, :, 0 : groups * ROWS] = lax.dot_general(
                jnp.broadcast_to(gates[e], (8, 256)).astype(BF16), selz[mz, e], NT, preferred_element_type=F32
            )

    def columns(k):
        return slice(k * width, (k + 1) * width)

    third = groups // 3

    parts = [pl.ds(p * third, third) for p in range(3)]

    def start_raw(k):
        b = B_CHUNKS.index(k)
        swap_done(k)
        for d in (1, 3):
            if k == B_CHUNKS[0]:
                send(x2.at[sib_rows, columns(k)], raw_z.at[b, mz, sib_rows], zr.at[k, d - 1], zdev[d], 3)
            else:
                send(x2.at[:, columns(k)], raw_z.at[b, mz], zr.at[k, d - 1], zdev[d], 3)

    def start_own(k):
        b = B_CHUNKS.index(k)
        cols = pl.ds(pl.multiple_of(mc * half + k * width, 128), width)
        for d in (1, 3):
            send(x_hbm.at[:, cols], raw_z.at[b, mz, mine_rows], zr.at[k, d - 1], zdev[d], 3)

    def relay_raw(k):
        b = B_CHUNKS.index(k)
        for d, part in ((1, pl.ds(0, 128)), (3, pl.ds(128, 128))):
            z = lax.rem(mz - d + NZ, NZ)
            arrived(raw_z.at[b, z], zr.at[k, d - 1])
            ref = raw_z.at[b, z, part]
            send(ref, ref, zr.at[k, 1], zdev[d], 3)

    def pack(k):
        a = A_CHUNKS.index(k)
        swap_done(k)
        for e in range(EXPERTS):
            block = jnp.dot(selz[mz, e], x2[:, columns(k)], preferred_element_type=F32)
            packed[a, e] = block.astype(BF16).reshape(groups, ROWS, width)

    locals_ = {}

    def start_x(k):
        if k == NC:
            locals_[k] = pltpu.make_async_copy(gs.at[mx], gt.at[mz, mx], loc_sem.at[k])
        elif k in A_CHUNKS:
            locals_[k] = pltpu.make_async_copy(
                packed.at[A_CHUNKS.index(k), mx], rows.at[k, mc, :, mz, mx], loc_sem.at[k]
            )
        else:
            locals_[k] = pltpu.make_async_copy(
                packed_z.at[B_CHUNKS.index(k), mx], rows.at[k, mc, :, :, mx], loc_sem.at[k]
            )
        locals_[k].start()
        for p, at in enumerate(parts if k in B_CHUNKS else parts[:1]):
            for d in (2, 1, 3):
                e = lax.rem(mx + d, NX)
                if k == NC:
                    send(gs.at[e], gt.at[mz, mx], xa.at[len(A_CHUNKS), d - 1], xdev[d], 6)
                elif k in A_CHUNKS:
                    a = A_CHUNKS.index(k)
                    send(packed.at[a, e], rows.at[k, mc, :, mz, mx], xa.at[a, d - 1], xdev[d], 0)
                else:
                    b = B_CHUNKS.index(k)
                    send(packed_z.at[b, e, at], rows.at[k, mc, at, :, mx], xb.at[b, d - 1, p], xdev[d], 1)

    def around_z(k):
        locals_[k].wait()
        for d in (1, 2, 3):
            x = lax.rem(mx - d + NX, NX)
            a = len(A_CHUNKS) if k == NC else A_CHUNKS.index(k)
            arrived(gt.at[mz, x] if k == NC else rows.at[k, mc, :, mz, x], xa.at[a, d - 1])
        if k == NC:
            for d in (1, 3, 2):
                send(gt.at[mz], gt.at[mz], zr.at[k, d - 1], zdev[d], 7)
            return
        ref = rows.at[k, mc, :, mz]
        for d in (1, 3):
            send(ref, ref, zr.at[k, d - 1], zdev[d], 2)
        send(ref, ref, br.at[k, 0], sibling, 4)

    def cross_x(k):
        b = B_CHUNKS.index(k)
        opposite = lax.rem(mz + 2, NZ)
        arrived(raw_z.at[b, opposite], zr.at[k, 1])
        for d in range(NZ):
            z = lax.rem(mz + d, NZ)
            tokens = raw_z[b, z] if d else x2[:, columns(k)]
            for e in range(EXPERTS):
                block = jnp.dot(selz[z, e], tokens, preferred_element_type=F32)
                packed_z[b, e, :, z] = block.astype(BF16).reshape(groups, ROWS, width)
        start_x(k)

    def near(k):
        for d, share in ((1, pl.ds(0, 2)), (3, pl.ds(2, 2))):
            z = lax.rem(mz - d + NZ, NZ)
            arrived(rows.at[k, mc, :, z], zr.at[k, d - 1])
            ref = rows.at[k, mc, :, z, share]
            send(ref, ref, zr.at[k, 1], zdev[d], 2)

    def near_shared(k):
        for d in (1, 3):
            ref = rows.at[k, mc, :, lax.rem(mz - d + NZ, NZ)]
            send(ref, ref, br.at[k, 0], sibling, 4)

    def far(k):
        ref = rows.at[k, mc, :, lax.rem(mz + 2, NZ)]
        arrived(ref, zr.at[k, 1])
        send(ref, ref, br.at[k, 0], sibling, 4)

    def whole(step):
        k, p = step % 100, step // 100 - 1
        b, at = B_CHUNKS.index(k), parts[p]
        if p == 0:
            locals_[k].wait()
        for d in (1, 2, 3):
            arrived(rows.at[k, mc, at, :, lax.rem(mx - d + NX, NX)], xb.at[b, d - 1, p])
        send(rows.at[k, mc, at], rows.at[k, mc, at], br.at[k, p if k == THIRDS else 0], sibling, 4)

    def shared(k):
        arrived(rows.at[k, 1 - mc], br.at[k, 0])

    def terms(ks, at):
        total = None
        for k in ks:
            slot = ORDER.index(k) % HELD
            for h in range(2):
                left = rows[k, h, at].reshape(third * 256, width)
                term = lax.dot_general(left, wv[slot, h], NT, preferred_element_type=F32)
                total = term if total is None else total + term
        return total.reshape(third, 256, total.shape[-1])

    def w_ready(k):
        slot = ORDER.index(k) % HELD
        pltpu.make_async_copy(wv.at[slot], wv.at[slot], w_sem.at[slot]).wait()

    def compute(step):
        if step >= 100:
            k, p = step % 100, step // 100 - 1
            arrived(rows.at[k, 1 - mc, parts[p]], br.at[k, p])
            if p == 0:
                w_ready(k)
            acc[parts[p]] += terms((k,), parts[p])
            return
        ks = PASSES[step]
        for k in ks:
            shared(k)
            w_ready(k)

        def body(m, carry):
            at = pl.ds(m * third, third)
            total = terms(ks, at)
            acc[at] = total if step == 0 else acc[at] + total
            return carry

        lax.fori_loop(0, 3, body, 0)
        for k in ks:
            later = ORDER.index(k) + HELD
            if later < len(ORDER):
                for copy in w_copies(ORDER[later]):
                    copy.start()

    def in_order(names):
        steps = {
            "u": start_own, "t": start_raw, "r": relay_raw, "c": cross_x, "g": own_select, "p": pack, "x": start_x, "a": around_z,
            "n": near, "f": far, "w": whole, "m": compute, "s": near_shared,
        }
        for word in names:
            steps[word[0]](int(word[1:]))

    in_order(FIRST)
    around_z(NC)
    for d in (1, 2, 3):
        z = lax.rem(mz + d, NZ)
        arrived(info.at[z], zr.at[NC + 1, NZ - d - 1])
        select(z)
    in_order(EARLY)
    perm = permutation(False)

    def place_saved(g, carry):
        sv[g] = jnp.dot(perm, sv[g], preferred_element_type=F32).astype(BF16)
        return carry

    arrived(next_ids, b0_recv.at[4])
    arrived(next_logits, b0_recv.at[5])
    code, gate = codes_of(next_ids, next_logits, mc.astype(F32))
    next_gate[...] = gate
    row = lax.broadcasted_iota(jnp.int32, (groups * ROWS, 128), 0).astype(F32)
    for e in range(EXPERTS):
        next_sel[e] = (row == code[e : e + 1]).astype(F32)
    for copy in s_copy:
        copy.wait()
    lax.fori_loop(0, groups, place_saved, 0)
    for d in (1, 2, 3):
        arrived(gt.at[lax.rem(mz - d + NZ, NZ)], zr.at[NC, d - 1])
    in_order(LATE)
    lane = lax.broadcasted_iota(jnp.int32, (256, 256), 1)
    row16 = lax.broadcasted_iota(jnp.int32, (256, 256), 0) & 15

    shared(ORDER[-1])
    w_ready(ORDER[-1])

    def dots(m, total):
        at = pl.ds(m * third, third)
        raw = acc[at] + terms(ORDER[-1:], at)
        acc[at] = raw
        part = jnp.sum(raw * sv[at].astype(F32), axis=2, keepdims=True)
        for n in range(third):
            placed = jnp.where(lane == row16 + (m * third + n) * 16, part[n], 0.0)
            total = total + jnp.sum(placed.reshape(16, 16, 256), axis=1)
        return total

    part = lax.fori_loop(0, 3, dots, jnp.zeros((16, 256), F32))
    pts[...] = jnp.broadcast_to(part[:, None, :], (16, 8, 256))
    slot = mx * NZ + mz
    own_part = pltpu.make_async_copy(pts.at[mz * NX + mx], pr.at[slot], loc_sem.at[NC + 1])
    own_part.start()
    for n, (dx, dz) in enumerate(chips):
        x, z = lax.rem(mx + dx, NX), lax.rem(mz + dz, NZ)
        send(pts.at[z * NX + x], pr.at[slot], pr_sem.at[n], dev(x, z, mc), 9)

    gates = jnp.broadcast_to(gt[...].reshape(16, 8, 256)[:, 0:1, :], (16, 16, 256)).reshape(256, 256)

    back = permutation(True)

    def finish(g, carry):
        gate = jnp.sum(jnp.where(lane == row16 + g * 16, gates, 0.0), axis=1, keepdims=True)
        grad = (gate * acc[g]).astype(BF16)
        sv[g] = jnp.dot(back, grad, preferred_element_type=F32).astype(BF16)
        pltpu.make_async_copy(sv.at[g], grad_hbm.at[g], o_sem.at[0]).start()
        return carry

    lax.fori_loop(0, groups, finish, 0)

    own_part.wait()
    for n, (dx, dz) in enumerate(chips):
        x, z = lax.rem(mx - dx + NX, NX), lax.rem(mz - dz + NZ, NZ)
        arrived(pr.at[x * NZ + z], pr_sem.at[n])
    summed = jnp.sum(pr[...].reshape(EXPERTS, NZ, 8, 256), axis=1)
    sums[...] = summed
    send(sums, next_sums.at[mc], next_sem.at[mc], before, 16)
    send(sums, next_sums.at[mc], next_sem.at[mc], before_other, 16)
    pltpu.make_async_copy(sv, grad_hbm, o_sem.at[0]).wait()
    arrived(next_hbm, b0_recv.at[2])
    arrived(nrouter_hbm, b0_recv.at[3])
    arrived(next_sums.at[0], next_sem.at[0])
    arrived(next_sums.at[1], next_sem.at[1])
    total = next_sums[0] + next_sums[1]
    token = [
        jnp.dot(total[e, :, 0 : groups * ROWS], next_sel[e], preferred_element_type=F32, precision=HIGHEST)[0:1]
        for e in range(EXPERTS)
    ]
    token = jnp.concatenate(token * 2, axis=0)
    gate = next_gate[...]
    mixed = jnp.sum((gate * token)[0:EXPERTS], axis=0, keepdims=True)
    spread_ref[...] = gate * (token - mixed)
    three = pl.ds(0, 3)
    na = len(A_CHUNKS)
    for kind, ref in enumerate(
        (
            packed.at[:, three], packed_z.at[:, three], rows.at[pl.ds(0, na), 0, :, three], raw_z.at[:, three],
            rows.at[:, 0], info.at[three], gs.at[three], gt.at[three], x2.at[pl.ds(0, 128), :], pts.at[pl.ds(0, 15)],
            info.at[0, 0], logits.at[0], next_hbm, nrouter_hbm, next_logits, next_ids, next_sums,
        )
    ):
        drain(ref, kind)


def expert_call(tokens, ids, logits, saved, weight, router):
    depth, hidden = tokens.shape[-1], weight.shape[0]
    groups = saved.shape[0]
    width = depth // 2 // NC
    dma = pltpu.SemaphoreType.DMA
    anywhere = pl.BlockSpec(memory_space=pl.ANY)
    na, nb = len(A_CHUNKS), len(B_CHUNKS)
    return pl.pallas_call(
        functools.partial(expert_kernel, groups, width),
        name="experts",
        out_shape=(
            jax.ShapeDtypeStruct((groups, 256, hidden), BF16),
            jax.ShapeDtypeStruct(tokens.shape, BF16),
            jax.ShapeDtypeStruct(router.shape, F32),
            jax.ShapeDtypeStruct((8, 128), F32),
        ),
        in_specs=[anywhere] * 6,
        out_specs=(anywhere, anywhere, anywhere, pl.BlockSpec(memory_space=pltpu.VMEM)),
        scratch_shapes=[
            pltpu.VMEM((NC, 2, groups, NZ, NX, ROWS, width), BF16),
            pltpu.VMEM((HELD, 2, hidden, width), BF16),
            pltpu.VMEM((groups, 256, hidden), F32),
            pltpu.VMEM((groups, 256, hidden), BF16),
            pltpu.VMEM((256, depth // 2), BF16),
            pltpu.VMEM((NZ, 2) + ids.shape, jnp.int32),
            pltpu.VMEM((2,) + ids.shape, F32),
            pltpu.VMEM((NZ, EXPERTS, groups * ROWS, 256), BF16),
            pltpu.VMEM((na, EXPERTS, groups, ROWS, width), BF16),
            pltpu.VMEM((nb, NZ, 256, width), BF16),
            pltpu.VMEM((nb, EXPERTS, groups, NZ, ROWS, width), BF16),
            pltpu.VMEM((EXPERTS, 8, 256), F32),
            pltpu.VMEM((NZ, NX, 8, 256), F32),
            pltpu.VMEM((8, 128), F32),
            pltpu.VMEM((EXPERTS, groups * ROWS, 128), F32),
            pltpu.VMEM(ids.shape, jnp.int32),
            pltpu.VMEM(ids.shape, F32),
            pltpu.VMEM((16, 8, 256), F32),
            pltpu.VMEM((16, 8, 256), F32),
            pltpu.VMEM((EXPERTS, 8, 256), F32),
            pltpu.VMEM((2, EXPERTS, 8, 256), F32),
            dma((PIECES + 2,)), dma((HELD,)), dma((1,)), dma((1,)), dma((NC + 2,)), dma((17,)), dma((6 + PIECES,)),
            dma((na + 1, 3)), dma((nb, 3, 3)), dma((NC + 2, 3)), dma((NC, 3)), dma((15,)), dma((2,)),
        ],
        compiler_params=pltpu.CompilerParams(
            collective_id=0, has_side_effects=True, vmem_limit_bytes=67043328
        ),
        cost_estimate=pl.CostEstimate(
            flops=2 * groups * 256 * depth * hidden, bytes_accessed=200_000_000, transcendentals=0
        ),
    )(tokens, ids, logits, saved, weight, router)


def last_kernel(
    grad_hbm, tokens_hbm, router_ref, spread_ref, hidden_hbm, upstream_hbm,
    grad, tokens, upstream, grad_in, grad_out, token_in, token_out,
):
    groups, pieces = grad.shape[0], tokens.shape[0]
    width = tokens.shape[2]
    reads, token_reads, writes = [], [], []
    for q in range(pieces):
        cols = pl.ds(q * width, width)
        token_reads.append(pltpu.make_async_copy(tokens_hbm.at[:, cols], tokens.at[q], token_in.at[q]))
        token_reads[q].start()
    for g in range(groups):
        reads.append(pltpu.make_async_copy(grad_hbm.at[g], grad.at[g], grad_in.at[g]))
        reads[g].start()

    def write(src, dst, sem):
        writes.append(pltpu.make_async_copy(src, dst, sem))
        writes[-1].start()

    live = lax.axis_index("section") < lax.axis_size("section") - 1
    spread = jnp.transpose(spread_ref[...])
    for q in range(pieces):
        token_reads[q].wait()
        total = tokens[q].astype(F32)
        for e in range(EXPERTS):
            total = total + spread[:, e : e + 1] * router_ref[e : e + 1, q * width : (q + 1) * width]
        upstream[q] = jnp.where(live, total, 0.0).astype(BF16)
        write(upstream.at[q], upstream_hbm.at[:, pl.ds(q * width, width)], token_out.at[q])
        for g in range(q * groups // pieces, (q + 1) * groups // pieces):
            reads[g].wait()
            write(grad.at[g], hidden_hbm.at[g], grad_out.at[g])
    for copy in writes:
        copy.wait()


def last_call(grad, tokens, router, spread):
    groups = grad.shape[0]
    flat, depth = tokens.shape
    pieces = 4
    anywhere = pl.BlockSpec(memory_space=pl.ANY)
    whole = pl.BlockSpec(memory_space=pltpu.VMEM)
    dma = pltpu.SemaphoreType.DMA
    return pl.pallas_call(
        last_kernel,
        name="last",
        out_shape=(jax.ShapeDtypeStruct(grad.shape, BF16), jax.ShapeDtypeStruct(tokens.shape, BF16)),
        in_specs=[anywhere, anywhere, whole, whole],
        out_specs=(anywhere, anywhere),
        scratch_shapes=[
            pltpu.VMEM(grad.shape, BF16),
            pltpu.VMEM((pieces, flat, depth // pieces), BF16),
            pltpu.VMEM((pieces, flat, depth // pieces), BF16),
            dma((groups,)), dma((groups,)), dma((pieces,)), dma((pieces,)),
        ],
        compiler_params=pltpu.CompilerParams(vmem_limit_bytes=67043328),
    )(grad, tokens, router, spread)


def local(upstream_dy, gate_logits, expert_ids, saved_hidden, down_weight, router_weight):
    micro, per, depth = upstream_dy.shape[1:]
    hidden = down_weight.shape[1]
    flat = micro * per
    saved = saved_hidden[0].transpose(0, 2, 1, 3).reshape(micro * CAP // 8, 256, hidden)
    grad, tokens, router, spread = expert_call(
        upstream_dy[0].reshape(flat, depth), expert_ids[0].transpose(0, 2, 1), gate_logits[0].transpose(0, 2, 1), saved, down_weight[0], router_weight[0].T
    )
    hidden_grad, upstream = last_call(grad, tokens, router, spread)
    hidden_grad = hidden_grad.reshape(micro, CAP, NX * NZ * 2, hidden).transpose(0, 2, 1, 3)
    return (hidden_grad[None], upstream.reshape(micro, per, depth)[None])


def solution(mesh):
    placed = (
        P("section", None, "expert", None),
        P("section", None, "expert", None),
        P("section", None, "expert", None),
        P("section", None, None, None, "expert"),
        P("section", "expert", None),
        P("section", None, None),
    )
    return jax.shard_map(
        local,
        mesh=mesh,
        in_specs=placed,
        out_specs=(P("section", None, None, None, "expert"), P("section", None, "expert", None)),
        check_vma=False,
    )
```
